256 devices in a mesh: prow: 16 (over x, y), pcol: 16 (over z, core).
Axes of the slice: x: 4, y: 4, z: 8, core: 2. Of those that a mesh axis runs over, the one named last changes fastest.
Arguments:
- ainv: float32 [16384, 16384], P('prow', 'pcol'), as said below
- panels: float32 [3, 16384, 512], P(None, 'prow', 'pcol'), may hold values from -0.53 to 0.53
- pattern: int32 [3, 128], replicated, may hold values 0 or 1
- coupling: float32 [3, 512, 512], replicated, may hold values from -0.25 to 0.25
- dinv: float32 [3, 512, 512], replicated, as said below
Outputs:
- xpanel: float32 [3, 16384, 512], P(None, 'prow', 'pcol')
- xcross: float32 [3, 512, 512], P(None, 'pcol')
- ydiag: float32 [3, 512, 512], P(None, 'pcol')
The draws below stay inside these ranges and needn't reach their ends.
Inputs may be any that keep to these rules, and one draw needn't show every extreme that they name: ainv is symmetric: ainv equals its transpose up to rounding. Each dinv[k] is symmetric: it equals its transpose exactly.
All inputs are finite; a program needn't handle non-finite values.
Results may differ from the reference program's by a relative error of at most 0.000092.
Values sent between devices are 32-bit elements; how exact they have to be, the bound alone decides.
A program may use at most 128 MiB of HBM per device.

```python
import jax
import jax.numpy as jnp
from jax import lax

NB = 128
W = 512
M = 16384
NBLK = 128


def draw_ainv(key, part):
    sample = jax.random.normal(jax.random.fold_in(key, 11), (M, M), jnp.float32)
    symmetric = (sample + sample.T) * 0.5 ** 0.5
    return jnp.clip(symmetric, -6.0, 6.0) * M ** (-0.5)


def draw_dinv(key, part):
    sample = jax.random.normal(jax.random.fold_in(key, 22), (3, W, W), jnp.float32) * 0.5
    symmetric = (sample + jnp.swapaxes(sample, 1, 2)) * 0.5 ** 0.5
    return jnp.clip(symmetric, -3.0, 3.0)


def set_ends(array, key, low, top_value):
    longest = array.shape.index(max(array.shape))
    spots = []
    for shift in (0, 1):
        where = [jax.random.randint(jax.random.fold_in(key, axis), (), 0, length) for axis, length in enumerate(array.shape)]
        where[longest] = (where[longest] + shift) % array.shape[longest]
        spots.append(tuple(where))
    return array.at[spots[0]].set(low).at[spots[1]].set(top_value)


def shard_levels(stream_key, extent, cuts, least, top_value):
    factor_of, own = 1.0, jax.random.fold_in(stream_key, 6)
    for dim, shards_of in cuts:
        draws = jnp.exp(jax.random.uniform(jax.random.fold_in(own, dim), (shards_of,), jnp.float32, least / len(cuts), top_value / len(cuts)))
        factor_of = factor_of * jnp.repeat(draws, extent[dim] // shards_of).reshape([-1 if axis == dim else 1 for axis in range(len(extent))])
    return factor_of


def gaussian(rng, dims, scale, reach, pieces=(), dtype=jnp.bfloat16):
    values = scale * jax.random.normal(rng, dims, jnp.float32)
    if pieces:
        values = values * shard_levels(rng, dims, pieces, -0.22, 0.18)
    return jnp.clip(values, -reach, reach).astype(dtype)


def setup_inputs(seed: int = 0) -> dict:
    keys = jax.random.split(jax.random.key(seed), 6)
    ainv = draw_ainv(jax.random.fold_in(keys[5], 71), 0)
    panels = gaussian(keys[1], (3, M, W), 0.088, 0.53, ((1, 16), (2, 16)), jnp.float32)
    pattern = set_ends((jax.random.randint(keys[2], (3, NBLK), 0, 4) < 3).astype(jnp.int32), jax.random.fold_in(keys[2], 1), 0, 1)
    coupling = gaussian(keys[3], (3, W, W), W ** -0.5, 0.25, (), jnp.float32)
    dinv = draw_dinv(jax.random.fold_in(keys[5], 71), 0)
    return {"ainv": ainv, "panels": panels, "pattern": pattern, "coupling": coupling, "dinv": dinv}


def matmul(left, right):
    return jnp.dot(left, right, precision=lax.Precision.HIGHEST, preferred_element_type=jnp.float32)


def tdot(left, right):
    return lax.dot_general(left, right, (((0,), (0,)), ((), ())), precision=lax.Precision.HIGHEST, preferred_element_type=jnp.float32)


def reference(ainv, panels, pattern, coupling, dinv):
    row_mask = jnp.repeat(pattern.astype(jnp.float32), NB, axis=1)
    factors = panels * row_mask[:, :, None]
    first, second, third = coupling[0], coupling[1], coupling[2]
    col_zero = -matmul(ainv, factors[0])
    col_one = -(matmul(ainv, factors[1]) + matmul(col_zero, first))
    col_two = -(matmul(ainv, factors[2]) + matmul(col_zero, second) + matmul(col_one, third))
    diag_zero = dinv[0] - tdot(factors[0], col_zero)
    cross_one = -(tdot(col_zero, factors[1]) + matmul(diag_zero, first))
    diag_one = dinv[1] - tdot(factors[1], col_one) - tdot(first, cross_one)
    cross_two = -(tdot(col_zero, factors[2]) + matmul(diag_zero, second) + matmul(cross_one, third))
    cross_three = -(tdot(col_one, factors[2]) + tdot(cross_one, second) + matmul(diag_one, third))
    diag_two = dinv[2] - tdot(factors[2], col_two) - tdot(second, cross_two) - tdot(third, cross_three)
    xpanel = jnp.stack([col_zero, col_one, col_two], 0)
    xcross = jnp.stack([cross_one, cross_two, cross_three], 0)
    ydiag = jnp.stack([diag_zero, diag_one, diag_two], 0)
    return (xpanel, xcross, ydiag)
```

```python
import jax
import jax.numpy as jnp
from jax import lax
from jax.sharding import PartitionSpec as P

NB = 128

high = lax.Precision.HIGH
highest = lax.Precision.HIGHEST


def mm(left, right, precision=high):
    return jnp.dot(left, right, precision=precision, preferred_element_type=jnp.float32)


def tmm(left, right, precision=high):
    return lax.dot_general(
        left, right, (((0,), (0,)), ((), ())), precision=precision, preferred_element_type=jnp.float32
    )


def mmt(left, right, precision=high):
    return lax.dot_general(
        left, right, (((1,), (1,)), ((), ())), precision=precision, preferred_element_type=jnp.float32
    )


def shards(ainv, panels, pattern, coupling, dinv):
    rows = lax.axis_size("prow")
    cols = lax.axis_size("pcol")
    row_index = lax.axis_index("prow")
    col_index = lax.axis_index("pcol")
    count, depth, width = panels.shape
    blocks_here = depth // NB
    flags = lax.dynamic_slice_in_dim(pattern, row_index * blocks_here, blocks_here, 1)
    row_mask = jnp.repeat(flags.astype(jnp.float32), NB, axis=1)
    factors = jnp.swapaxes(panels, 1, 2) * row_mask[:, None, :]
    f0, f1, f2 = lax.all_gather(factors, "pcol", axis=1, tiled=True)
    c0, c1, c2 = coupling[0], coupling[1], coupling[2]
    u01 = -c0
    u12 = -c2
    u02 = mm(c0, c2, highest) - c1
    h0 = f0
    h1 = f1 + tmm(u01, f0)
    h2 = f2 + tmm(u02, f0) + tmm(u12, f1)
    ht = jnp.concatenate([h0, h1, h2], 0)
    partial = mm(ht, ainv).reshape(count, rows, width, depth)
    mine = lax.psum_scatter(partial, "prow", scatter_dimension=1, tiled=False)
    perm = [(r * cols + c, c * cols + r) for r in range(rows) for c in range(cols)]
    xt = -lax.ppermute(mine, ("prow", "pcol"), perm)
    inner0 = mmt(xt[0], ht)
    inner1 = mmt(xt[1], ht[512:])
    inner2 = mmt(xt[2], ht[1024:])
    summed = lax.psum(jnp.concatenate([inner0, inner1, inner2], 1), "prow")
    start = col_index * width

    def own(matrix, axis):
        return lax.dynamic_slice_in_dim(matrix, start, width, axis)

    d0 = own(dinv[0], 0)
    a01 = tmm(own(u01, 1), dinv[0], highest)
    a02 = tmm(own(u02, 1), dinv[0], highest)
    b1 = own(dinv[1], 0)
    b12 = tmm(own(u12, 1), dinv[1], highest)
    y0 = d0 - summed[:, 0:512]
    e01 = mm(d0, u01, highest) - summed[:, 512:1024]
    e02 = mm(d0, u02, highest) - summed[:, 1024:1536]
    y1 = b1 + mm(a01, u01, highest) - summed[:, 1536:2048]
    e12 = mm(a01, u02, highest) + mm(b1, u12, highest) - summed[:, 2048:2560]
    y2 = own(dinv[2], 0) + mm(a02, u02, highest) + mm(b12, u12, highest) - summed[:, 2560:3072]
    return jnp.swapaxes(xt, 1, 2), jnp.stack([e01, e02, e12], 0), jnp.stack([y0, y1, y2], 0)


def solution(mesh):
    placed = (P("prow", "pcol"), P(None, "prow", "pcol"), P(), P(), P())
    return jax.shard_map(
        shards,
        mesh=mesh,
        in_specs=placed,
        out_specs=(P(None, "prow", "pcol"), P(None, "pcol", None), P(None, "pcol", None)),
        check_vma=False,
    )
```

```python
import functools

import jax
import jax.numpy as jnp
from jax import lax
from jax.experimental import pallas as pl
from jax.experimental.pallas import tpu as pltpu
from jax.sharding import PartitionSpec as P

NB = 128
F32 = jnp.float32
BF16 = jnp.bfloat16
MESH = pl.DeviceIdType.MESH
highest = lax.Precision.HIGHEST

NN = (((1,), (0,)), ((), ()))
NT = (((1,), (1,)), ((), ()))


def split(value):
    top = value.astype(BF16)
    return top, (value - top.astype(F32)).astype(BF16)


def dot(left, right, dims=NN):
    return lax.dot_general(left, right, dims, preferred_element_type=F32)


def exact(left, right, dims=NN):
    return lax.dot_general(left, right, dims, precision=highest, preferred_element_type=F32)


def lanes(index, size):
    return pl.ds(pl.multiple_of(index * size, 128), size)


def kernel(
    pan, pat, coup, dinv, ainv, xt_out, xc_out, yd_out,
    G, Hh, Hl, A32, Ah, Al, C32, D32, Ch, Cl, PX,
    RLX, FNX, RLY, FNY, RLX2, FNX2, RLY2, FNY2,
    XS, ZB, XF, IN0, IN1, IN2, RB0, RB1, RB2, OU0, OU1, OU2, VD,
    load_sem, ag_s, ag_r, pf_s, pf_r, rs_s, rs_r, za_s, za_r, xa_s, xa_r, ra_s, ra_r, ga_s, ga_r,
):
    r = lax.axis_index("prow")
    c = lax.axis_index("pcol")
    x, y = r // 4, r % 4
    z, core = c // 2, c % 2
    sends = []

    load_pan = pltpu.make_async_copy(pan, G.at[:, c], load_sem.at[0])
    load_a = pltpu.make_async_copy(ainv, A32, load_sem.at[1])
    load_c = pltpu.make_async_copy(coup, C32, load_sem.at[2])
    load_d = pltpu.make_async_copy(dinv, D32, load_sem.at[3])
    load_pan.start()
    load_a.start()
    load_c.start()
    load_d.start()

    barrier = pltpu.get_barrier_semaphore()

    def greet(o, carry):
        pl.semaphore_signal(barrier, inc=1, device_id={"pcol": (c + o) % 16}, device_id_type=MESH)
        pl.semaphore_signal(barrier, inc=1, device_id={"prow": (r + o) % 16}, device_id_type=MESH)
        return carry

    lax.fori_loop(1, 16, greet, 0)
    pl.semaphore_wait(barrier, 30)

    def remote(src, dst, send, recv, device):
        return pltpu.make_async_remote_copy(
            src_ref=src, dst_ref=dst, send_sem=send, recv_sem=recv, device_id=device, device_id_type=MESH
        )

    def start(copy):
        copy.start()
        sends.append(copy)

    def ag(d, k, e, t):
        chip = (z + 8 - t) % 8 if d == 0 else (z + t) % 8
        near = (z + 1) % 8 if d == 0 else (z + 7) % 8
        part = G.at[k, 2 * chip + core, pl.ds(16 * e, 16)]
        return remote(part, part, ag_s.at[d, k, e, t], ag_r.at[d, k, e, t], {"pcol": 2 * near + core})

    def pf(k, e, q):
        part = G.at[k, 2 * ((z + 8 - q) % 8) + core, pl.ds(16 * e, 16)]
        return remote(part, part, pf_s.at[k, e, q], pf_r.at[k, e, q], {"pcol": 2 * z + 1 - core})

    def travels(d, e, t):
        return t < 3 or (t == 3 and d == e)

    def ag_start(k):
        for e in range(2):
            for d in range(2):
                start(ag(d, k, e, 0))
        for e in range(2):
            start(pf(k, e, 0))

    def ag_step(k, t):
        for e in range(2):
            for d in range(2):
                if travels(d, e, t):
                    ag(d, k, e, t).wait_recv()
                    if travels(d, e, t + 1):
                        start(ag(d, k, e, t + 1))
                    start(pf(k, e, t + 1 if d == 0 else 7 - t))

    def ag_end(k):
        for e in range(2):
            for q in range(8):
                pf(k, e, q).wait_recv()

    def prep_a(part):
        def body(i, carry):
            rows = pl.ds(pl.multiple_of(i * 64, 64), 64)
            top, low = split(-A32[rows, :])
            Ah[rows, :] = top
            Al[rows, :] = low
            return carry

        lax.fori_loop(4 * part, 4 * part + 4, body, 0)

    def prep_c():
        def body(i, carry):
            for m in range(3):
                top, low = split(jnp.transpose(C32[m, :, lanes(i, 128)]))
                rows = pl.ds(pl.multiple_of(i * 128, 128), 128)
                Ch[m, rows, :] = top
                Cl[m, rows, :] = low
            return carry

        lax.fori_loop(0, 4, body, 0)

    def prep_d():
        own = pl.ds(pl.multiple_of(c * 32, 32), 32)
        row = lax.broadcasted_iota(jnp.int32, (32, 512), 0) + c * 32
        pick = (lax.broadcasted_iota(jnp.int32, (32, 512), 1) == row).astype(F32)
        c0p = exact(pick, C32[0], NT)
        c1p = exact(pick, C32[1], NT)
        c2p = exact(pick, C32[2], NT)
        d0, d1, d2 = D32[0, own, :], D32[1, own, :], D32[2, own, :]
        u02p = exact(c2p, C32[0], NT) - c1p
        ta = exact(jnp.concatenate([-c0p, u02p], 0), D32[0])
        t0 = jnp.concatenate([d0, ta], 0)
        t1 = exact(-c2p, D32[1])
        zero = jnp.zeros_like(d0)
        v1 = jnp.concatenate([zero, d1, t1], 0) - exact(t0, C32[0])
        v2 = jnp.concatenate([zero, zero, d2], 0) - exact(t0, C32[1]) - exact(v1, C32[2])
        VD[0] = d0
        VD[1] = v1[0:32]
        VD[2] = v2[0:32]
        VD[3] = v1[32:64]
        VD[4] = v2[32:64]
        VD[5] = v2[64:96]

    def comp_h(k):
        def body(j, carry):
            here = lanes(j, 256)
            first = pat[k, r * 8 + 2 * j].astype(F32)
            second = pat[k, r * 8 + 2 * j + 1].astype(F32)
            mask = jnp.where(lax.broadcasted_iota(jnp.int32, (1, 256), 1) < 128, first, second)
            value = G[k, :, :, here].reshape(512, 256) * mask
            for l in range(k):
                m = l if k == 1 else l + 1
                value = value - (
                    dot(Ch[m], Hh[l, :, here]) + dot(Cl[m], Hh[l, :, here]) + dot(Ch[m], Hl[l, :, here])
                )
            top, low = split(value)
            Hh[k, :, here] = top
            Hl[k, :, here] = low
            return carry

        lax.fori_loop(0, 4, body, 0)

    def comp_p(k, lo, hi):
        def body(j, carry):
            here = lanes(j, 256)
            value = dot(Hh[k], Ah[:, here]) + dot(Hh[k], Al[:, here]) + dot(Hl[k], Ah[:, here])
            PX[k, :, :, :, here] = value.reshape(16, 4, 8, 256)
            return carry

        lax.fori_loop(lo, hi, body, 0)

    class Ring:
        def __init__(self, k, phase, own, relay, final, me, device, out):
            self.own, self.relay, self.final, self.me, self.out = own, relay, final, me, out
            right, left = device((me + 1) % 4), device((me + 3) % 4)
            self.next, self.prev, self.far = (me + 1) % 4, (me + 3) % 4, (me + 2) % 4
            lower, upper = pl.ds(0, 4), pl.ds(4, 4)
            sem = lambda i: (rs_s.at[k, phase, i], rs_r.at[k, phase, i])
            self.relay_r = remote(own(self.far, 0), relay.at[0], *sem(0), right)
            self.relay_l = remote(own(self.far, 1), relay.at[1], *sem(1), left)
            self.raw_r = remote(own(self.next, 1), final.at[0, upper], *sem(2), right)
            self.raw_l = remote(own(self.prev, 0), final.at[1, lower], *sem(3), left)
            self.sum_r = remote(relay.at[0], final.at[0, lower], *sem(4), right)
            self.sum_l = remote(relay.at[1], final.at[1, upper], *sem(5), left)

        def start(self):
            for copy in (self.relay_r, self.relay_l, self.raw_r, self.raw_l):
                start(copy)

        def mid(self):
            for side, copy, chunk, onward in (
                (0, self.relay_r, self.next, self.sum_r),
                (1, self.relay_l, self.prev, self.sum_l),
            ):
                copy.wait_recv()
                mine = self.own(chunk, side)

                def body(i, carry):
                    self.relay[side, i] = self.relay[side, i] + mine[i]
                    return carry

                lax.fori_loop(0, 4, body, 0)
                start(onward)

        def end(self):
            for copy in (self.raw_r, self.raw_l, self.sum_r, self.sum_l):
                copy.wait_recv()
            for side in range(2):
                mine = self.own(self.me, side)
                into = self.out(side)

                def body(i, carry):
                    into[i] = mine[i] + self.final[0, 4 * side + i] + self.final[1, 4 * side + i]
                    return carry

                lax.fori_loop(0, 4, body, 0)

    along_x = lambda t: {"prow": t * 4 + y}
    along_y = lambda t: {"prow": x * 4 + t}

    def rings(k):
        def parts(base, h):
            return pl.ds(base + 4 * h, 4)

        own_x1 = lambda t, h: PX.at[k, parts(0, h), t]
        own_y1 = lambda t, h: PX.at[k, parts(8, h), :, :, lanes(t, 256)]
        own_x2 = lambda t, h: PX.at[k, parts(0, h), x, :, lanes(t, 256)]
        own_y2 = lambda t, h: PX.at[k, parts(8, h), t, :, lanes(y, 256)]
        first = (
            Ring(k, 0, own_x1, RLX.at[k], FNX.at[k], x, along_x, lambda h: own_x1(x, h)),
            Ring(k, 1, own_y1, RLY.at[k], FNY.at[k], y, along_y, lambda h: own_y1(y, h)),
        )
        second = (
            Ring(k, 2, own_x2, RLX2.at[k], FNX2.at[k], y, along_y, lambda h: XS.at[parts(0, h), k]),
            Ring(k, 3, own_y2, RLY2.at[k], FNY2.at[k], x, along_x, lambda h: XS.at[parts(8, h), k]),
        )
        return first, second

    ring = [rings(k) for k in range(3)]

    def rs_start(k, phase):
        for item in ring[k][phase]:
            item.start()

    def rs_mid(k, phase):
        for item in ring[k][phase]:
            item.mid()

    def rs_end(k, phase):
        for item in ring[k][phase]:
            item.end()

    def each(copy, action):
        def body(o, carry):
            getattr(copy(o), action)()
            return carry

        lax.fori_loop(1, 16, body, 0)

    loops = []

    def begin(copy):
        each(copy, "start")
        loops.append(copy)

    def za(k):
        def copy(o):
            to = (c + o) % 16
            return remote(XS.at[to, k], ZB.at[c, k], za_s.at[k, o], za_r.at[k, o], {"pcol": to})

        return copy

    def xa(k):
        def copy(o):
            to = (r + o) % 16
            return remote(
                ZB.at[to, k], XF.at[k, x, :, lanes(y, 256)], xa_s.at[k, o], xa_r.at[k, o], {"prow": to}
            )

        return copy

    def za_start(k):
        begin(za(k))
        ZB[c, k] = XS[c, k]

    def xa_start(k):
        each(za(k), "wait_recv")
        begin(xa(k))
        XF[k, x, :, lanes(y, 256)] = ZB[r, k]

    def xa_end(k):
        each(xa(k), "wait_recv")

    IN, RB, OU = (IN0, IN1, IN2), (RB0, RB1, RB2), (OU0, OU1, OU2)

    def inner(k):
        value = XF[k].reshape(32, 1024)
        xt_out[k] = value
        top, low = split(value)
        both = jnp.concatenate([top, low], 0)
        for m in range(k, 3):
            wide = dot(both, Hh[m], NT)
            total = wide[0:32] + wide[32:64] + dot(top, Hl[m], NT)
            IN[k][:, :, pl.ds((m - k) * 512, 512)] = total.reshape(4, 8, 512)

    def ra(k):
        w = 128 * (3 - k)

        def copy(o):
            to = (r + o) % 16
            return remote(
                IN[k].at[to // 4, :, lanes(to % 4, w)], RB[k].at[o], ra_s.at[k, o], ra_r.at[k, o], {"prow": to}
            )

        return copy

    def ga(k):
        w = 128 * (3 - k)
        mine = OU[k].at[x, :, lanes(y, w)]

        def copy(o):
            return remote(mine, mine, ga_s.at[k, o], ga_r.at[k, o], {"prow": (r + o) % 16})

        return copy

    def ar_start(k):
        inner(k)
        begin(ra(k))

    def ar_mid(k):
        w = 128 * (3 - k)
        each(ra(k), "wait_recv")
        total = IN[k][x, :, lanes(y, w)]
        for o in range(1, 16):
            total = total + RB[k][o]
        OU[k][x, :, lanes(y, w)] = total
        begin(ga(k))

    def ar_end(k):
        each(ga(k), "wait_recv")
        places = (((yd_out, 0), (xc_out, 0), (xc_out, 1)), ((yd_out, 1), (xc_out, 2)), ((yd_out, 2),))[k]
        first = (0, 3, 5)[k]
        for i, (target, slot) in enumerate(places):
            got = OU[k][:, :, pl.ds(i * 512, 512)].reshape(32, 512)
            target[slot] = VD[first + i] - got

    load_pan.wait()
    ag_start(0)
    load_a.wait()
    prep_a(0)
    prep_a(1)
    ag_step(0, 0)
    prep_a(2)
    prep_a(3)
    ag_step(0, 1)
    load_c.wait()
    prep_c()
    ag_step(0, 2)
    ag_start(1)
    ag_step(0, 3)
    ag_end(0)
    comp_h(0)
    ag_step(1, 0)
    comp_p(0, 0, 2)
    ag_step(1, 1)
    comp_p(0, 2, 4)
    rs_start(0, 0)
    ag_step(1, 2)
    ag_start(2)
    load_d.wait()
    prep_d()
    ag_step(1, 3)
    rs_mid(0, 0)
    ag_end(1)
    comp_h(1)
    ag_step(2, 0)
    comp_p(1, 0, 2)
    rs_end(0, 0)
    rs_start(0, 1)
    ag_step(2, 1)
    comp_p(1, 2, 4)
    rs_start(1, 0)
    rs_mid(0, 1)
    ag_step(2, 2)
    ag_step(2, 3)
    rs_end(0, 1)
    za_start(0)
    rs_mid(1, 0)
    ag_end(2)
    comp_h(2)
    xa_start(0)
    comp_p(2, 0, 2)
    rs_end(1, 0)
    rs_start(1, 1)
    xa_end(0)
    ar_start(0)
    comp_p(2, 2, 4)
    rs_start(2, 0)
    rs_mid(1, 1)
    ar_mid(0)
    rs_end(1, 1)
    za_start(1)
    rs_mid(2, 0)
    xa_start(1)
    ar_end(0)
    xa_end(1)
    ar_start(1)
    rs_end(2, 0)
    rs_start(2, 1)
    ar_mid(1)
    rs_mid(2, 1)
    rs_end(2, 1)
    za_start(2)
    ar_end(1)
    xa_start(2)
    xa_end(2)
    ar_start(2)
    ar_mid(2)
    ar_end(2)

    for copy in sends:
        copy.wait_send()
    for copy in loops:
        each(copy, "wait_send")


def scratch():
    v = pltpu.VMEM
    sem = pltpu.SemaphoreType.DMA
    return [
        v((3, 16, 32, 1024), F32), v((3, 512, 1024), BF16), v((3, 512, 1024), BF16),
        v((1024, 1024), F32), v((1024, 1024), BF16), v((1024, 1024), BF16),
        v((3, 512, 512), F32), v((3, 512, 512), F32), v((3, 512, 512), BF16), v((3, 512, 512), BF16),
        v((3, 16, 4, 8, 1024), F32),
        v((3, 2, 4, 8, 1024), F32), v((3, 2, 8, 8, 1024), F32),
        v((3, 2, 4, 4, 8, 256), F32), v((3, 2, 8, 4, 8, 256), F32),
        v((3, 2, 4, 8, 256), F32), v((3, 2, 8, 8, 256), F32),
        v((3, 2, 4, 8, 256), F32), v((3, 2, 8, 8, 256), F32),
        v((16, 3, 8, 256), F32), v((16, 3, 8, 256), F32), v((3, 4, 8, 1024), F32),
        v((4, 8, 1536), F32), v((4, 8, 1024), F32), v((4, 8, 512), F32),
        v((16, 8, 384), F32), v((16, 8, 256), F32), v((16, 8, 128), F32),
        v((4, 8, 1536), F32), v((4, 8, 1024), F32), v((4, 8, 512), F32),
        v((6, 32, 512), F32),
        sem((4,)), sem((2, 3, 2, 4)), sem((2, 3, 2, 4)), sem((3, 2, 8)), sem((3, 2, 8)),
        sem((3, 4, 6)), sem((3, 4, 6)),
        sem((3, 16)), sem((3, 16)), sem((3, 16)), sem((3, 16)),
        sem((3, 16)), sem((3, 16)), sem((3, 16)), sem((3, 16)),
    ]


def shards(ainv, panels, pattern, coupling, dinv):
    any_space = pl.BlockSpec(memory_space=pl.ANY)
    vmem = pl.BlockSpec(memory_space=pltpu.VMEM)
    xt, xc, yd = pl.pallas_call(
        kernel,
        out_shape=(
            jax.ShapeDtypeStruct((3, 32, 1024), F32),
            jax.ShapeDtypeStruct((3, 32, 512), F32),
            jax.ShapeDtypeStruct((3, 32, 512), F32),
        ),
        in_specs=[any_space, pl.BlockSpec(memory_space=pltpu.SMEM), any_space, any_space, any_space],
        out_specs=(vmem, vmem, vmem),
        scratch_shapes=scratch(),
        compiler_params=pltpu.CompilerParams(
            collective_id=0, has_side_effects=True, vmem_limit_bytes=64 * 1024 * 1024 - 65536
        ),
    )(jnp.swapaxes(panels, 1, 2), pattern, coupling, dinv, ainv)
    return jnp.swapaxes(xt, 1, 2), xc, yd


def solution(mesh):
    placed = (P("prow", "pcol"), P(None, "prow", "pcol"), P(), P(), P())
    return jax.shard_map(
        shards,
        mesh=mesh,
        in_specs=placed,
        out_specs=(P(None, "prow", "pcol"), P(None, "pcol", None), P(None, "pcol", None)),
        check_vma=False,
    )
```

```python
import jax
import jax.numpy as jnp
from jax import lax
from jax.experimental import pallas as pl
from jax.experimental.pallas import tpu as pltpu
from jax.sharding import PartitionSpec as P

NB = 128
F32 = jnp.float32
BF16 = jnp.bfloat16
MESH = pl.DeviceIdType.MESH

NN = (((1,), (0,)), ((), ()))
NT = (((1,), (1,)), ((), ()))


def split(value):
    top = value.astype(BF16)
    return top, (value - top.astype(F32)).astype(BF16)


def dot(left, right, dims=NN):
    return lax.dot_general(left, right, dims, preferred_element_type=F32)


def lanes(index, size):
    return pl.ds(pl.multiple_of(index * size, 128), size)


def kernel(
    pan, pat, coup, dinv, ainv, xt_out, xc_out, yd_out,
    G, Hh, Hl, A32, Ah, Al, C32, D32, Ch, Cl, RM, PX,
    RLX, FNX, RLY, FNY, RLX2, FNX2, RLY2, FNY2,
    XS, ZB, XF, IN0, IN1, IN2, RB0, RB1, RB2, OU0, OU1, OU2, VD,
    load_sem, ag_r, pf_r, rs_r, za_r, xa_r, ra_r, ga_r, sent,
):
    r = lax.axis_index("prow")
    c = lax.axis_index("pcol")
    x, y = r // 4, r % 4
    z, core = c // 2, c % 2

    load_pan = pltpu.make_async_copy(pan, G.at[:, c], load_sem.at[0])
    load_a = pltpu.make_async_copy(ainv, A32, load_sem.at[1])
    load_c = pltpu.make_async_copy(coup, C32, load_sem.at[2])
    load_d = pltpu.make_async_copy(dinv, D32, load_sem.at[3])
    load_pan.start()
    load_a.start()
    load_c.start()
    load_d.start()

    barrier = pltpu.get_barrier_semaphore()

    for near in (2 * ((z + 1) % 8) + core, 2 * ((z + 7) % 8) + core, 2 * z + 1 - core):
        pl.semaphore_signal(barrier, inc=1, device_id={"pcol": near}, device_id_type=MESH)
    for near in (x * 4 + (y + 1) % 4, x * 4 + (y + 3) % 4, (x + 1) % 4 * 4 + y, (x + 3) % 4 * 4 + y):
        pl.semaphore_signal(barrier, inc=1, device_id={"prow": near}, device_id_type=MESH)
    pl.semaphore_wait(barrier, 7)

    def remote(src, dst, send, recv, device):
        return pltpu.make_async_remote_copy(
            src_ref=src, dst_ref=dst, send_sem=send, recv_sem=recv, device_id=device, device_id_type=MESH
        )

    def take(ref, semaphore):
        pltpu.make_async_copy(ref, ref, semaphore).wait()

    def ag(d, k, e, t):
        chip = (z + 8 - t) % 8 if d == 0 else (z + t) % 8
        near = (z + 1) % 8 if d == 0 else (z + 7) % 8
        part = G.at[k, 2 * chip + core, pl.ds(8 * e, 8)]
        return remote(part, part, sent.at[0], ag_r.at[d, k, e, t], {"pcol": 2 * near + core})

    def pf(k, e, q):
        part = G.at[k, 2 * ((z + 8 - q) % 8) + core, pl.ds(8 * e, 8)]
        return remote(part, part, sent.at[1], pf_r.at[k], {"pcol": 2 * z + 1 - core})

    def travels(d, e, t):
        return t < 3 or (t == 3 and d == e // 2)

    def ag_start(k):
        for e in range(4):
            for d in range(2):
                ag(d, k, e, 0).start()
        for e in range(4):
            pf(k, e, 0).start()

    def ag_step(k, t):
        for e in range(4):
            for d in range(2):
                if travels(d, e, t):
                    ag(d, k, e, t).wait_recv()
                    if travels(d, e, t + 1):
                        ag(d, k, e, t + 1).start()
                    pf(k, e, t + 1 if d == 0 else 7 - t).start()

    def ag_end(k):
        take(G.at[k, pl.ds(0, 8)], pf_r.at[k])

    def prep_a(part):
        def body(i, carry):
            rows = pl.ds(pl.multiple_of(i * 64, 64), 64)
            top, low = split(-A32[rows, :])
            Ah[rows, :] = top
            Al[rows, :] = low
            return carry

        lax.fori_loop(4 * part, 4 * part + 4, body, 0)

    def prep_c():
        def body(i, carry):
            for m in range(3):
                top, low = split(jnp.transpose(C32[m, :, lanes(i, 128)]))
                rows = pl.ds(pl.multiple_of(i * 128, 128), 128)
                Ch[m, rows, :] = top
                Cl[m, rows, :] = low
            return carry

        lax.fori_loop(0, 4, body, 0)

    def triple(left, top, low, dims=NN):
        n = left.shape[0]
        a, b = split(left)
        wide = dot(jnp.concatenate([a, b], 0), top, dims)
        return wide[0:n] + wide[n:] + dot(a, low, dims)

    def prep_d():
        own = pl.ds(pl.multiple_of(c * 32, 32), 32)
        c0p, c1p, c2p = (Ch[m, own, :].astype(F32) + Cl[m, own, :].astype(F32) for m in range(3))
        d0, d1, d2 = D32[0, own, :], D32[1, own, :], D32[2, own, :]
        u02p = triple(c2p, Ch[0], Cl[0]) - c1p
        t0 = jnp.concatenate([d0, triple(jnp.concatenate([-c0p, u02p], 0), *split(D32[0]))], 0)
        t1 = triple(-c2p, *split(D32[1]))
        zero = jnp.zeros_like(d0)
        v1 = jnp.concatenate([zero, d1, t1], 0) - triple(t0, Ch[0], Cl[0], NT)
        v2 = jnp.concatenate([zero, zero, d2], 0) - triple(t0, Ch[1], Cl[1], NT) - triple(v1, Ch[2], Cl[2], NT)
        VD[0] = d0
        VD[1] = v1[0:32]
        VD[2] = v2[0:32]
        VD[3] = v1[32:64]
        VD[4] = v2[32:64]
        VD[5] = v2[64:96]

    def comp_r(k, lo, hi):
        def body(j, carry):
            here = lanes(j, 256)
            value = jnp.zeros((512, 256), F32)
            for l in range(k):
                m = l if k == 1 else l + 1
                value = value + (
                    dot(Ch[m], Hh[l, :, here]) + dot(Cl[m], Hh[l, :, here]) + dot(Ch[m], Hl[l, :, here])
                )
            RM[:, here] = value
            return carry

        lax.fori_loop(lo, hi, body, 0)

    def comp_h(k):
        def body(j, carry):
            here = lanes(j, 256)
            first = pat[k, r * 8 + 2 * j].astype(F32)
            second = pat[k, r * 8 + 2 * j + 1].astype(F32)
            mask = jnp.where(lax.broadcasted_iota(jnp.int32, (1, 256), 1) < 128, first, second)
            value = G[k, :, :, here].reshape(512, 256) * mask
            if k > 0:
                value = value - RM[:, here]
            top, low = split(value)
            Hh[k, :, here] = top
            Hl[k, :, here] = low
            return carry

        lax.fori_loop(0, 4, body, 0)

    def comp_p(k, half):
        rows = pl.ds(256 * half, 256)

        def body(j, carry):
            here = lanes(j, 256)
            top, low = Hh[k, rows, :], Hl[k, rows, :]
            value = dot(top, Ah[:, here]) + dot(low, Ah[:, here]) + dot(top, Al[:, here])
            PX[k, pl.ds(8 * half, 8), :, :, here] = value.reshape(8, 4, 8, 256)
            return carry

        lax.fori_loop(0, 4, body, 0)

    class Ring:
        def __init__(self, k, phase, own, relay, final, me, device, out):
            self.own, self.relay, self.final, self.me, self.out = own, relay, final, me, out
            right, left = device((me + 1) % 4), device((me + 3) % 4)
            self.next, self.prev, self.far = (me + 1) % 4, (me + 3) % 4, (me + 2) % 4
            lower, upper = pl.ds(0, 4), pl.ds(4, 4)
            self.done = rs_r.at[k, phase, 2]
            sem = lambda i: (sent.at[2], rs_r.at[k, phase, i])
            self.relay_r = remote(own(self.far, 0), relay.at[0], *sem(0), right)
            self.relay_l = remote(own(self.far, 1), relay.at[1], *sem(1), left)
            self.raw_r = remote(own(self.next, 1), final.at[0, upper], *sem(2), right)
            self.raw_l = remote(own(self.prev, 0), final.at[1, lower], *sem(2), left)
            self.sum_r = remote(relay.at[0], final.at[0, lower], *sem(2), right)
            self.sum_l = remote(relay.at[1], final.at[1, upper], *sem(2), left)

        def start(self):
            for copy in (self.relay_r, self.relay_l, self.raw_r, self.raw_l):
                copy.start()

        def mid(self):
            for side, copy, chunk, onward in (
                (0, self.relay_r, self.next, self.sum_r),
                (1, self.relay_l, self.prev, self.sum_l),
            ):
                copy.wait_recv()
                mine = self.own(chunk, side)

                def body(i, carry):
                    self.relay[side, i] = self.relay[side, i] + mine[i]
                    return carry

                lax.fori_loop(0, 4, body, 0)
                onward.start()

        def end(self):
            take(self.final, self.done)
            for side in range(2):
                mine = self.own(self.me, side)
                into = self.out(side)

                def body(i, carry):
                    into[i] = mine[i] + self.final[0, 4 * side + i] + self.final[1, 4 * side + i]
                    return carry

                lax.fori_loop(0, 4, body, 0)

    along_x = lambda t: {"prow": t * 4 + y}
    along_y = lambda t: {"prow": x * 4 + t}

    def rings(k):
        def parts(base, h):
            return pl.ds(base + 4 * h, 4)

        own_x1 = lambda t, h: PX.at[k, parts(0, h), t]
        own_y1 = lambda t, h: PX.at[k, parts(8, h), :, :, lanes(t, 256)]
        own_x2 = lambda t, h: PX.at[k, parts(0, h), x, :, lanes(t, 256)]
        own_y2 = lambda t, h: PX.at[k, parts(8, h), t, :, lanes(y, 256)]
        first = (
            Ring(k, 0, own_x1, RLX.at[k], FNX.at[k], x, along_x, lambda h: own_x1(x, h)),
            Ring(k, 1, own_y1, RLY.at[k], FNY.at[k], y, along_y, lambda h: own_y1(y, h)),
        )
        second = (
            Ring(k, 2, own_x2, RLX2.at[k], FNX2.at[k], y, along_y, lambda h: XS.at[parts(0, h), k]),
            Ring(k, 3, own_y2, RLY2.at[k], FNY2.at[k], x, along_x, lambda h: XS.at[parts(8, h), k]),
        )
        return first, second

    ring = [rings(k) for k in range(3)]

    def rs_start(k, phase, *which):
        for i in which or (0, 1):
            ring[k][phase][i].start()

    def rs_mid(k, phase):
        for item in ring[k][phase]:
            item.mid()

    def rs_end(k, phase):
        for item in ring[k][phase]:
            item.end()

    def begin(copy):
        def body(o, carry):
            copy(o).start()
            return carry

        lax.fori_loop(1, 16, body, 0)

    def za(k):
        def copy(o):
            to = (c + o) % 16
            return remote(XS.at[to, k], ZB.at[c, k], sent.at[3], za_r.at[k], {"pcol": to})

        return copy

    def xa(k):
        def copy(o):
            to = (r + o) % 16
            return remote(
                ZB.at[to, k], XF.at[k, x, :, lanes(y, 256)], sent.at[4], xa_r.at[k], {"prow": to}
            )

        return copy

    def za_start(k):
        begin(za(k))
        ZB[c, k] = XS[c, k]

    def xa_start(k):
        take(ZB.at[pl.ds(0, 15), k], za_r.at[k])
        begin(xa(k))
        XF[k, x, :, lanes(y, 256)] = ZB[r, k]

    def xa_end(k):
        take(ZB.at[pl.ds(0, 15), k], xa_r.at[k])

    IN, RB, OU = (IN0, IN1, IN2), (RB0, RB1, RB2), (OU0, OU1, OU2)

    def inner(k):
        value = XF[k].reshape(32, 1024)
        xt_out[k] = value
        top, low = split(value)
        both = jnp.concatenate([top, low], 0)
        for m in range(k, 3):
            wide = dot(both, Hh[m], NT)
            total = wide[0:32] + wide[32:64] + dot(top, Hl[m], NT)
            IN[k][:, :, pl.ds((m - k) * 512, 512)] = total.reshape(4, 8, 512)

    def ra(k):
        w = 128 * (3 - k)

        def copy(o):
            to = (r + o) % 16
            return remote(
                IN[k].at[to // 4, :, lanes(to % 4, w)], RB[k].at[o], sent.at[5], ra_r.at[k], {"prow": to}
            )

        return copy

    def ga(k):
        w = 128 * (3 - k)
        mine = OU[k].at[x, :, lanes(y, w)]

        def copy(o):
            return remote(mine, mine, sent.at[6], ga_r.at[k], {"prow": (r + o) % 16})

        return copy

    def ar_start(k):
        inner(k)
        begin(ra(k))

    def ar_mid(k):
        w = 128 * (3 - k)
        take(RB[k].at[pl.ds(1, 15)], ra_r.at[k])
        total = IN[k][x, :, lanes(y, w)]
        for o in range(1, 16):
            total = total + RB[k][o]
        OU[k][x, :, lanes(y, w)] = total
        begin(ga(k))

    def ar_end(k):
        take(RB[k].at[pl.ds(1, 15)], ga_r.at[k])
        places = (((yd_out, 0), (xc_out, 0), (xc_out, 1)), ((yd_out, 1), (xc_out, 2)), ((yd_out, 2),))[k]
        first = (0, 3, 5)[k]
        for i, (target, slot) in enumerate(places):
            got = OU[k][:, :, pl.ds(i * 512, 512)].reshape(32, 512)
            target[slot] = VD[first + i] - got

    load_pan.wait()
    ag_start(0)
    load_a.wait()
    prep_a(0)
    prep_a(1)
    ag_step(0, 0)
    prep_a(2)
    prep_a(3)
    load_c.wait()
    prep_c()
    ag_step(0, 1)
    load_d.wait()
    prep_d()
    ag_step(0, 2)
    ag_start(1)
    ag_step(0, 3)
    ag_end(0)
    comp_h(0)
    comp_p(0, 0)
    rs_start(0, 0, 0)
    ag_step(1, 0)
    comp_p(0, 1)
    rs_start(0, 0, 1)
    ag_step(1, 1)
    comp_r(1, 0, 4)
    rs_mid(0, 0)
    ag_step(1, 2)
    ag_start(2)
    ag_step(1, 3)
    ag_end(1)
    comp_h(1)
    comp_p(1, 0)
    rs_end(0, 0)
    rs_start(0, 1)
    rs_start(1, 0, 0)
    ag_step(2, 0)
    comp_p(1, 1)
    rs_start(1, 0, 1)
    ag_step(2, 1)
    comp_r(2, 0, 2)
    rs_mid(0, 1)
    rs_mid(1, 0)
    ag_step(2, 2)
    comp_r(2, 2, 4)
    ag_step(2, 3)
    rs_end(0, 1)
    za_start(0)
    ag_end(2)
    comp_h(2)
    comp_p(2, 0)
    rs_start(2, 0, 0)
    comp_p(2, 1)
    rs_start(2, 0, 1)
    xa_start(0)
    rs_end(1, 0)
    rs_start(1, 1)
    xa_end(0)
    ar_start(0)
    rs_mid(1, 1)
    rs_mid(2, 0)
    rs_end(1, 1)
    za_start(1)
    ar_mid(0)
    rs_end(2, 0)
    rs_start(2, 1)
    xa_start(1)
    rs_mid(2, 1)
    xa_end(1)
    ar_start(1)
    rs_end(2, 1)
    za_start(2)
    ar_end(0)
    ar_mid(1)
    xa_start(2)
    ar_end(1)
    xa_end(2)
    ar_start(2)
    ar_mid(2)
    ar_end(2)

    for i, ref in enumerate((
        G.at[:, pl.ds(0, 7)], G.at[:, pl.ds(0, 8)], PX.at[:, pl.ds(0, 15)],
        ZB.at[pl.ds(0, 15)], ZB.at[pl.ds(0, 15)], ZB.at[pl.ds(0, 15)], ZB.at[pl.ds(0, 15)],
    )):
        take(ref, sent.at[i])


def finish(xt, xc, yd, xt_out, xc_out, yd_out, a, b, c, inward, outward):
    trips = []
    for i, (source, held, target) in enumerate(((xt, a, xt_out), (xc, b, xc_out), (yd, c, yd_out))):
        arrive = pltpu.make_async_copy(source, held, inward.at[i])
        arrive.start()
        trips.append((arrive, pltpu.make_async_copy(held, target, outward.at[i])))
    for arrive, leave in trips:
        arrive.wait()
        leave.start()
    for arrive, leave in trips:
        leave.wait()


def scratch():
    v = pltpu.VMEM
    sem = pltpu.SemaphoreType.DMA
    return [
        v((3, 16, 32, 1024), F32), v((3, 512, 1024), BF16), v((3, 512, 1024), BF16),
        v((1024, 1024), F32), v((1024, 1024), BF16), v((1024, 1024), BF16),
        v((3, 512, 512), F32), v((3, 512, 512), F32), v((3, 512, 512), BF16), v((3, 512, 512), BF16),
        v((512, 1024), F32),
        v((3, 16, 4, 8, 1024), F32),
        v((3, 2, 4, 8, 1024), F32), v((3, 2, 8, 8, 1024), F32),
        v((3, 2, 4, 4, 8, 256), F32), v((3, 2, 8, 4, 8, 256), F32),
        v((3, 2, 4, 8, 256), F32), v((3, 2, 8, 8, 256), F32),
        v((3, 2, 4, 8, 256), F32), v((3, 2, 8, 8, 256), F32),
        v((16, 3, 8, 256), F32), v((16, 3, 8, 256), F32), v((3, 4, 8, 1024), F32),
        v((4, 8, 1536), F32), v((4, 8, 1024), F32), v((4, 8, 512), F32),
        v((16, 8, 384), F32), v((16, 8, 256), F32), v((16, 8, 128), F32),
        v((4, 8, 1536), F32), v((4, 8, 1024), F32), v((4, 8, 512), F32),
        v((6, 32, 512), F32),
        sem((4,)), sem((2, 3, 4, 4)), sem((3,)), sem((3, 4, 3)),
        sem((3,)), sem((3,)), sem((3,)), sem((3,)), sem((7,)),
    ]


def shards(ainv, panels, pattern, coupling, dinv):
    any_space = pl.BlockSpec(memory_space=pl.ANY)
    vmem = pl.BlockSpec(memory_space=pltpu.VMEM)
    shapes = ((3, 32, 1024), (3, 32, 512), (3, 32, 512))
    results = tuple(jax.ShapeDtypeStruct(shape, F32) for shape in shapes)
    held = pl.pallas_call(
        kernel,
        out_shape=results,
        in_specs=[any_space, pl.BlockSpec(memory_space=pltpu.SMEM), any_space, any_space, any_space],
        out_specs=(vmem, vmem, vmem),
        scratch_shapes=scratch(),
        compiler_params=pltpu.CompilerParams(
            collective_id=0, has_side_effects=True, vmem_limit_bytes=64 * 1024 * 1024 - 65536
        ),
    )(jnp.swapaxes(panels, 1, 2), pattern, coupling, dinv, ainv)
    xt, xc, yd = pl.pallas_call(
        finish,
        out_shape=results,
        in_specs=[any_space] * 3,
        out_specs=(any_space,) * 3,
        scratch_shapes=[pltpu.VMEM(shape, F32) for shape in shapes] + [pltpu.SemaphoreType.DMA((3,))] * 2,
    )(*held)
    return jnp.swapaxes(xt, 1, 2), xc, yd


def solution(mesh):
    placed = (P("prow", "pcol"), P(None, "prow", "pcol"), P(), P(), P())
    return jax.shard_map(
        shards,
        mesh=mesh,
        in_specs=placed,
        out_specs=(P(None, "prow", "pcol"), P(None, "pcol", None), P(None, "pcol", None)),
        check_vma=False,
    )
```

```python
import jax
import jax.numpy as jnp
from jax import lax
from jax.experimental import pallas as pl
from jax.experimental.pallas import tpu as pltpu
from jax.sharding import PartitionSpec as P

NB = 128
F32 = jnp.float32
BF16 = jnp.bfloat16
MESH = pl.DeviceIdType.MESH

NN = (((1,), (0,)), ((), ()))
NT = (((1,), (1,)), ((), ()))


def split(value):
    top = value.astype(BF16)
    return top, (value - top.astype(F32)).astype(BF16)


def dot(left, right, dims=NN):
    return lax.dot_general(left, right, dims, preferred_element_type=F32)


def lanes(index, size):
    return pl.ds(pl.multiple_of(index * size, 128), size)


def kernel(
    pan, pat, coup, dinv, ainv, xt_out, xc_out, yd_out,
    G, HS, A32, Ah, Al, C32, D32, Ch, Cl, RM, PX,
    RLX, FNX, RLY, FNY, RLX2, FNX2, RLY2, FNY2,
    XS, ZB, XF, IN0, IN1, IN2, RB0, RB1, RB2, OU0, OU1, OU2, VD,
    load_sem, ag_r, pf_r, rs_r, za_r, xa_r, ra_r, ga_r, sent,
):
    r = lax.axis_index("prow")
    c = lax.axis_index("pcol")
    x, y = r // 4, r % 4
    z, core = c // 2, c % 2

    load_pan = pltpu.make_async_copy(pan, G.at[:, c], load_sem.at[0])
    load_a = pltpu.make_async_copy(ainv, A32, load_sem.at[1])
    load_c = pltpu.make_async_copy(coup, C32, load_sem.at[2])
    load_d = pltpu.make_async_copy(dinv, D32, load_sem.at[3])
    load_pan.start()
    load_a.start()
    load_c.start()
    load_d.start()

    barrier = pltpu.get_barrier_semaphore()

    for near in (2 * ((z + 1) % 8) + core, 2 * ((z + 7) % 8) + core, 2 * z + 1 - core):
        pl.semaphore_signal(barrier, inc=1, device_id={"pcol": near}, device_id_type=MESH)
    for near in (x * 4 + (y + 1) % 4, x * 4 + (y + 3) % 4, (x + 1) % 4 * 4 + y, (x + 3) % 4 * 4 + y):
        pl.semaphore_signal(barrier, inc=1, device_id={"prow": near}, device_id_type=MESH)
    pl.semaphore_wait(barrier, 7)

    def remote(src, dst, send, recv, device):
        return pltpu.make_async_remote_copy(
            src_ref=src, dst_ref=dst, send_sem=send, recv_sem=recv, device_id=device, device_id_type=MESH
        )

    def take(ref, semaphore):
        pltpu.make_async_copy(ref, ref, semaphore).wait()

    def ag(d, k, e, t):
        chip = (z + 8 - t) % 8 if d == 0 else (z + t) % 8
        near = (z + 1) % 8 if d == 0 else (z + 7) % 8
        part = G.at[k, 2 * chip + core, pl.ds(8 * e, 8)]
        return remote(part, part, sent.at[0], ag_r.at[d, k, e, t], {"pcol": 2 * near + core})

    def pf(k, e, q):
        part = G.at[k, 2 * ((z + 8 - q) % 8) + core, pl.ds(8 * e, 8)]
        return remote(part, part, sent.at[1], pf_r.at[k], {"pcol": 2 * z + 1 - core})

    def travels(d, e, t):
        return t < 3 or (t == 3 and d == e // 2)

    def ag_start(k):
        for e in range(4):
            for d in range(2):
                ag(d, k, e, 0).start()
        for e in range(4):
            pf(k, e, 0).start()

    def ag_step(k, t):
        for e in range(4):
            for d in range(2):
                if travels(d, e, t):
                    ag(d, k, e, t).wait_recv()
                    pf(k, e, t + 1 if d == 0 else 7 - t).start()
                    if travels(d, e, t + 1):
                        ag(d, k, e, t + 1).start()

    def ag_end(k):
        take(G.at[k, pl.ds(0, 8)], pf_r.at[k])

    def prep_a(part):
        def body(i, carry):
            rows = pl.ds(pl.multiple_of(i * 64, 64), 64)
            top, low = split(-A32[rows, :])
            Ah[rows, :] = top
            Al[rows, :] = low
            return carry

        lax.fori_loop(4 * part, 4 * part + 4, body, 0)

    def prep_c():
        def body(i, carry):
            for m in range(3):
                top, low = split(jnp.transpose(C32[m, :, lanes(i, 128)]))
                rows = pl.ds(pl.multiple_of(i * 128, 128), 128)
                Ch[m, rows, :] = top
                Cl[m, rows, :] = low
            return carry

        lax.fori_loop(0, 4, body, 0)

    def triple(left, top, low, dims=NN):
        n = left.shape[0]
        a, b = split(left)
        wide = dot(jnp.concatenate([a, b], 0), top, dims)
        return wide[0:n] + wide[n:] + dot(a, low, dims)

    def prep_d():
        own = pl.ds(pl.multiple_of(c * 32, 32), 32)
        c0p, c1p, c2p = (Ch[m, own, :].astype(F32) + Cl[m, own, :].astype(F32) for m in range(3))
        d0, d1, d2 = D32[0, own, :], D32[1, own, :], D32[2, own, :]
        u02p = triple(c2p, Ch[0], Cl[0]) - c1p
        t0 = jnp.concatenate([d0, triple(jnp.concatenate([-c0p, u02p], 0), *split(D32[0]))], 0)
        t1 = triple(-c2p, *split(D32[1]))
        zero = jnp.zeros_like(d0)
        v1 = jnp.concatenate([zero, d1, t1], 0) - triple(t0, Ch[0], Cl[0], NT)
        v2 = jnp.concatenate([zero, zero, d2], 0) - triple(t0, Ch[1], Cl[1], NT) - triple(v1, Ch[2], Cl[2], NT)
        VD[0] = d0
        VD[1] = v1[0:32]
        VD[2] = v2[0:32]
        VD[3] = v1[32:64]
        VD[4] = v2[32:64]
        VD[5] = v2[64:96]

    def comp_r(k, lo, hi):
        def body(j, carry):
            here = lanes(j, 256)
            value = jnp.zeros((512, 256), F32)
            for l in range(k):
                m = l if k == 1 else l + 1
                for h in range(2):
                    deep = pl.ds(256 * h, 256)
                    top, low = HS[l, h, pl.ds(0, 256), here], HS[l, h, pl.ds(256, 256), here]
                    left = Ch[m, :, deep]
                    value = value + (dot(left, top) + dot(Cl[m, :, deep], top) + dot(left, low))
            RM[:, here] = value
            return carry

        lax.fori_loop(lo, hi, body, 0)

    def comp_h(k):
        def body(j, carry):
            here = lanes(j, 256)
            first = pat[k, r * 8 + 2 * j].astype(F32)
            second = pat[k, r * 8 + 2 * j + 1].astype(F32)
            mask = jnp.where(lax.broadcasted_iota(jnp.int32, (1, 256), 1) < 128, first, second)
            value = G[k, :, :, here].reshape(512, 256) * mask
            if k > 0:
                value = value - RM[:, here]
            top, low = split(value)
            for h in range(2):
                HS[k, h, pl.ds(0, 256), here] = top[256 * h : 256 * h + 256]
                HS[k, h, pl.ds(256, 256), here] = low[256 * h : 256 * h + 256]
            return carry

        lax.fori_loop(0, 4, body, 0)

    def comp_all(k, lo, hi):
        def body(j, carry):
            here = lanes(j, 256)
            for h in range(2):
                wide = dot(HS[k, h], Ah[:, here])
                value = wide[0:256] + wide[256:512] + dot(HS[k, h, pl.ds(0, 256), :], Al[:, here])
                PX[k, pl.ds(8 * h, 8), :, :, here] = value.reshape(8, 4, 8, 256)
            return carry

        lax.fori_loop(lo, hi, body, 0)

    def comp_p(k, half, lo, hi):
        def body(j, carry):
            here = lanes(j, 256)
            wide = dot(HS[k, half], Ah[:, here])
            value = wide[0:256] + wide[256:512] + dot(HS[k, half, pl.ds(0, 256), :], Al[:, here])
            PX[k, pl.ds(8 * half, 8), :, :, here] = value.reshape(8, 4, 8, 256)
            return carry

        lax.fori_loop(lo, hi, body, 0)

    class Ring:
        def __init__(self, k, phase, own, relay, final, me, device, out):
            self.own, self.relay, self.final, self.me, self.out = own, relay, final, me, out
            right, left = device((me + 1) % 4), device((me + 3) % 4)
            self.next, self.prev, self.far = (me + 1) % 4, (me + 3) % 4, (me + 2) % 4
            lower, upper = pl.ds(0, 4), pl.ds(4, 4)
            self.done = rs_r.at[k, phase, 2]
            sem = lambda i: (sent.at[2], rs_r.at[k, phase, i])
            self.relay_r = remote(own(self.far, 0), relay.at[0], *sem(0), right)
            self.relay_l = remote(own(self.far, 1), relay.at[1], *sem(1), left)
            self.raw_r = remote(own(self.next, 1), final.at[0, upper], *sem(2), right)
            self.raw_l = remote(own(self.prev, 0), final.at[1, lower], *sem(2), left)
            self.sum_r = remote(relay.at[0], final.at[0, lower], *sem(2), right)
            self.sum_l = remote(relay.at[1], final.at[1, upper], *sem(2), left)

        def start(self):
            for copy in (self.relay_r, self.relay_l, self.raw_r, self.raw_l):
                copy.start()

        def mid(self):
            for side, copy, chunk, onward in (
                (0, self.relay_r, self.next, self.sum_r),
                (1, self.relay_l, self.prev, self.sum_l),
            ):
                copy.wait_recv()
                mine = self.own(chunk, side)

                def body(i, carry):
                    self.relay[side, i] = self.relay[side, i] + mine[i]
                    return carry

                lax.fori_loop(0, 4, body, 0)
                onward.start()

        def end(self):
            take(self.final, self.done)
            for side in range(2):
                mine = self.own(self.me, side)
                into = self.out(side)

                def body(i, carry):
                    into[i] = mine[i] + self.final[0, 4 * side + i] + self.final[1, 4 * side + i]
                    return carry

                lax.fori_loop(0, 4, body, 0)

    along_x = lambda t: {"prow": t * 4 + y}
    along_y = lambda t: {"prow": x * 4 + t}

    def rings(k):
        def parts(base, h):
            return pl.ds(base + 4 * h, 4)

        own_x1 = lambda t, h: PX.at[k, parts(0, h), t]
        own_y1 = lambda t, h: PX.at[k, parts(8, h), :, :, lanes(t, 256)]
        own_x2 = lambda t, h: PX.at[k, parts(0, h), x, :, lanes(t, 256)]
        own_y2 = lambda t, h: PX.at[k, parts(8, h), t, :, lanes(y, 256)]
        first = (
            Ring(k, 0, own_x1, RLX.at[k], FNX.at[k], x, along_x, lambda h: own_x1(x, h)),
            Ring(k, 1, own_y1, RLY.at[k], FNY.at[k], y, along_y, lambda h: own_y1(y, h)),
        )
        second = (
            Ring(k, 2, own_x2, RLX2.at[k], FNX2.at[k], y, along_y, lambda h: XS.at[parts(0, h), k]),
            Ring(k, 3, own_y2, RLY2.at[k], FNY2.at[k], x, along_x, lambda h: XS.at[parts(8, h), k]),
        )
        return first, second

    ring = [rings(k) for k in range(3)]

    def rs_start(k, phase, *which):
        for i in which or (0, 1):
            ring[k][phase][i].start()

    def rs_mid(k, phase, *which):
        for i in which or (0, 1):
            ring[k][phase][i].mid()

    def rs_end(k, phase, *which):
        for i in which or (0, 1):
            ring[k][phase][i].end()

    def begin(copy):
        def body(o, carry):
            copy(o).start()
            return carry

        lax.fori_loop(1, 16, body, 0)

    def za(k):
        def copy(o):
            to = (c + o) % 16
            return remote(XS.at[to, k], ZB.at[c, k], sent.at[3], za_r.at[k], {"pcol": to})

        return copy

    def xa(k):
        def copy(o):
            to = (r + o) % 16
            return remote(
                ZB.at[to, k], XF.at[k, x, :, lanes(y, 256)], sent.at[4], xa_r.at[k], {"prow": to}
            )

        return copy

    def za_start(k):
        begin(za(k))
        ZB[c, k] = XS[c, k]

    def xa_start(k):
        take(ZB.at[pl.ds(0, 15), k], za_r.at[k])
        begin(xa(k))
        XF[k, x, :, lanes(y, 256)] = ZB[r, k]

    def xa_end(k):
        take(ZB.at[pl.ds(0, 15), k], xa_r.at[k])

    IN, RB, OU = (IN0, IN1, IN2), (RB0, RB1, RB2), (OU0, OU1, OU2)

    def inner(k):
        value = XF[k].reshape(32, 1024)
        xt_out[k] = value
        top, low = split(value)
        both = jnp.concatenate([top, low], 0)
        for m in range(k, 3):
            for h in range(2):
                wide = dot(both, HS[m, h, pl.ds(0, 256), :], NT)
                total = wide[0:32] + wide[32:64] + dot(top, HS[m, h, pl.ds(256, 256), :], NT)
                IN[k][:, :, pl.ds((m - k) * 512 + 256 * h, 256)] = total.reshape(4, 8, 256)

    def ra(k):
        w = 128 * (3 - k)

        def copy(o):
            to = (r + o) % 16
            return remote(
                IN[k].at[to // 4, :, lanes(to % 4, w)], RB[k].at[o], sent.at[5], ra_r.at[k], {"prow": to}
            )

        return copy

    def ga(k):
        w = 128 * (3 - k)
        mine = OU[k].at[x, :, lanes(y, w)]

        def copy(o):
            return remote(mine, mine, sent.at[6], ga_r.at[k], {"prow": (r + o) % 16})

        return copy

    def ar_start(k):
        inner(k)
        begin(ra(k))

    def ar_mid(k):
        w = 128 * (3 - k)
        take(RB[k].at[pl.ds(1, 15)], ra_r.at[k])
        total = IN[k][x, :, lanes(y, w)]
        for o in range(1, 16):
            total = total + RB[k][o]
        OU[k][x, :, lanes(y, w)] = total
        begin(ga(k))

    def ar_end(k):
        take(RB[k].at[pl.ds(1, 15)], ga_r.at[k])
        places = (((yd_out, 0), (xc_out, 0), (xc_out, 1)), ((yd_out, 1), (xc_out, 2)), ((yd_out, 2),))[k]
        first = (0, 3, 5)[k]
        for i, (target, slot) in enumerate(places):
            got = OU[k][:, :, pl.ds(i * 512, 512)].reshape(32, 512)
            target[slot] = VD[first + i] - got

    load_pan.wait()
    ag_start(0)
    load_a.wait()
    prep_a(0)
    prep_a(1)
    ag_step(0, 0)
    prep_a(2)
    prep_a(3)
    load_c.wait()
    prep_c()
    ag_step(0, 1)
    ag_start(1)
    load_d.wait()
    prep_d()
    ag_step(0, 2)
    ag_step(1, 0)
    ag_step(0, 3)
    ag_start(2)
    ag_end(0)
    comp_h(0)
    ag_step(1, 1)
    comp_all(0, 0, 2)
    ag_step(2, 0)
    comp_all(0, 2, 4)
    rs_start(0, 0)
    ag_step(1, 2)
    comp_r(1, 0, 4)
    ag_step(2, 1)
    ag_step(1, 3)
    rs_mid(0, 0)
    ag_end(1)
    comp_h(1)
    comp_all(1, 0, 2)
    ag_step(2, 2)
    comp_all(1, 2, 4)
    rs_end(0, 0)
    rs_start(0, 1)
    rs_start(1, 0)
    comp_r(2, 0, 2)
    ag_step(2, 3)
    rs_mid(0, 1)
    comp_r(2, 2, 4)
    ag_end(2)
    comp_h(2)
    comp_p(2, 0, 0, 2)
    rs_mid(1, 0)
    comp_p(2, 0, 2, 4)
    rs_start(2, 0, 0)
    comp_p(2, 1, 0, 4)
    rs_start(2, 0, 1)
    rs_end(0, 1)
    za_start(0)
    rs_end(1, 0)
    rs_start(1, 1)
    rs_mid(2, 0)
    xa_start(0)
    rs_mid(1, 1)
    rs_end(2, 0, 0)
    rs_start(2, 1, 0)
    rs_end(2, 0, 1)
    rs_start(2, 1, 1)
    rs_end(1, 1)
    za_start(1)
    rs_mid(2, 1)
    xa_end(0)
    rs_end(2, 1)
    za_start(2)
    ar_start(0)
    xa_start(1)
    xa_start(2)
    xa_end(1)
    ar_start(1)
    ar_mid(0)
    xa_end(2)
    ar_start(2)
    ar_mid(1)
    ar_end(0)
    ar_mid(2)
    ar_end(1)
    ar_end(2)

    for i, ref in enumerate((
        G.at[:, pl.ds(0, 7)], G.at[:, pl.ds(0, 8)], PX.at[:, pl.ds(0, 15)],
        ZB.at[pl.ds(0, 15)], ZB.at[pl.ds(0, 15)], ZB.at[pl.ds(0, 15)], ZB.at[pl.ds(0, 15)],
    )):
        take(ref, sent.at[i])


def finish(xt, xc, yd, xt_out, xc_out, yd_out, a, b, c, inward, outward):
    trips = []
    for i, (source, held, target) in enumerate(((xt, a, xt_out), (xc, b, xc_out), (yd, c, yd_out))):
        arrive = pltpu.make_async_copy(source, held, inward.at[i])
        arrive.start()
        trips.append((arrive, pltpu.make_async_copy(held, target, outward.at[i])))
    for arrive, leave in trips:
        arrive.wait()
        leave.start()
    for arrive, leave in trips:
        leave.wait()


def scratch():
    v = pltpu.VMEM
    sem = pltpu.SemaphoreType.DMA
    return [
        v((3, 16, 32, 1024), F32), v((3, 2, 512, 1024), BF16),
        v((1024, 1024), F32), v((1024, 1024), BF16), v((1024, 1024), BF16),
        v((3, 512, 512), F32), v((3, 512, 512), F32), v((3, 512, 512), BF16), v((3, 512, 512), BF16),
        v((512, 1024), F32),
        v((3, 16, 4, 8, 1024), F32),
        v((3, 2, 4, 8, 1024), F32), v((3, 2, 8, 8, 1024), F32),
        v((3, 2, 4, 4, 8, 256), F32), v((3, 2, 8, 4, 8, 256), F32),
        v((3, 2, 4, 8, 256), F32), v((3, 2, 8, 8, 256), F32),
        v((3, 2, 4, 8, 256), F32), v((3, 2, 8, 8, 256), F32),
        v((16, 3, 8, 256), F32), v((16, 3, 8, 256), F32), v((3, 4, 8, 1024), F32),
        v((4, 8, 1536), F32), v((4, 8, 1024), F32), v((4, 8, 512), F32),
        v((16, 8, 384), F32), v((16, 8, 256), F32), v((16, 8, 128), F32),
        v((4, 8, 1536), F32), v((4, 8, 1024), F32), v((4, 8, 512), F32),
        v((6, 32, 512), F32),
        sem((4,)), sem((2, 3, 4, 4)), sem((3,)), sem((3, 4, 3)),
        sem((3,)), sem((3,)), sem((3,)), sem((3,)), sem((7,)),
    ]


def shards(ainv, panels, pattern, coupling, dinv):
    any_space = pl.BlockSpec(memory_space=pl.ANY)
    vmem = pl.BlockSpec(memory_space=pltpu.VMEM)
    shapes = ((3, 32, 1024), (3, 32, 512), (3, 32, 512))
    results = tuple(jax.ShapeDtypeStruct(shape, F32) for shape in shapes)
    held = pl.pallas_call(
        kernel,
        out_shape=results,
        in_specs=[any_space, pl.BlockSpec(memory_space=pltpu.SMEM), any_space, any_space, any_space],
        out_specs=(vmem, vmem, vmem),
        scratch_shapes=scratch(),
        compiler_params=pltpu.CompilerParams(
            collective_id=0, has_side_effects=True, vmem_limit_bytes=64 * 1024 * 1024 - 65536
        ),
    )(jnp.swapaxes(panels, 1, 2), pattern, coupling, dinv, ainv)
    xt, xc, yd = pl.pallas_call(
        finish,
        out_shape=results,
        in_specs=[any_space] * 3,
        out_specs=(any_space,) * 3,
        scratch_shapes=[pltpu.VMEM(shape, F32) for shape in shapes] + [pltpu.SemaphoreType.DMA((3,))] * 2,
    )(*held)
    return jnp.swapaxes(xt, 1, 2), xc, yd


def solution(mesh):
    placed = (P("prow", "pcol"), P(None, "prow", "pcol"), P(), P(), P())
    return jax.shard_map(
        shards,
        mesh=mesh,
        in_specs=placed,
        out_specs=(P(None, "prow", "pcol"), P(None, "pcol", None), P(None, "pcol", None)),
        check_vma=False,
    )
```

```python
import jax
import jax.numpy as jnp
from jax import lax
from jax.experimental import pallas as pl
from jax.experimental.pallas import tpu as pltpu
from jax.sharding import PartitionSpec as P

NB = 128
F32 = jnp.float32
BF16 = jnp.bfloat16
MESH = pl.DeviceIdType.MESH

NN = (((1,), (0,)), ((), ()))
NT = (((1,), (1,)), ((), ()))


def split(value):
    top = value.astype(BF16)
    return top, (value - top.astype(F32)).astype(BF16)


def dot(left, right, dims=NN):
    return lax.dot_general(left, right, dims, preferred_element_type=F32)


def lanes(index, size):
    return pl.ds(pl.multiple_of(index * size, 128), size)


def kernel(
    pan, pat, coup, dinv, ainv, xt_out, xc_out, yd_out,
    G, HS, flags, A32, Ah, Al, C32, D32, Ch, Cl, RM, PXX, PYY,
    RLX, FNX, RLY, FNY, RLX2, FNX2, RLY2, FNY2,
    XS, ZB, XF, IN0, IN1, IN2, RB0, RB1, RB2, OU0, OU1, OU2, VD,
    load_sem, ag_r, pf_r, rs_r, za_r, xa_r, ra_r, ga_r, sent,
):
    r = lax.axis_index("prow")
    c = lax.axis_index("pcol")
    x, y = r // 4, r % 4
    z, core = c // 2, c % 2

    load_pan = pltpu.make_async_copy(pan, G.at[:, c], load_sem.at[0])
    load_a = pltpu.make_async_copy(ainv, A32, load_sem.at[1])
    load_c = pltpu.make_async_copy(coup, C32, load_sem.at[2])
    load_d = pltpu.make_async_copy(dinv, D32, load_sem.at[3])
    load_f = pltpu.make_async_copy(pat, flags, load_sem.at[4])
    load_pan.start()

    barrier = pltpu.get_barrier_semaphore()

    for near in (2 * ((z + 1) % 8) + core, 2 * ((z + 7) % 8) + core, 2 * z + 1 - core):
        pl.semaphore_signal(barrier, inc=1, device_id={"pcol": near}, device_id_type=MESH)
    for near in (x * 4 + (y + 1) % 4, x * 4 + (y + 3) % 4, (x + 1) % 4 * 4 + y, (x + 3) % 4 * 4 + y):
        pl.semaphore_signal(barrier, inc=1, device_id={"prow": near}, device_id_type=MESH)
    pl.semaphore_wait(barrier, 7)

    def remote(src, dst, send, recv, device):
        return pltpu.make_async_remote_copy(
            src_ref=src, dst_ref=dst, send_sem=send, recv_sem=recv, device_id=device, device_id_type=MESH
        )

    def take(ref, semaphore):
        pltpu.make_async_copy(ref, ref, semaphore).wait()

    def ag(d, k, e, t):
        chip = (z + 8 - t) % 8 if d == 0 else (z + t) % 8
        near = (z + 1) % 8 if d == 0 else (z + 7) % 8
        part = G.at[k, 2 * chip + core, pl.ds(8 * e, 8)]
        return remote(part, part, sent.at[0], ag_r.at[d, k, e, t], {"pcol": 2 * near + core})

    def pf(k, e, q):
        part = G.at[k, 2 * ((z + 8 - q) % 8) + core, pl.ds(8 * e, 8)]
        return remote(part, part, sent.at[1], pf_r.at[k], {"pcol": 2 * z + 1 - core})

    def travels(d, e, t):
        return t < 3 or (t == 3 and d == e // 2)

    def ag_start(k):
        for e in range(4):
            for d in range(2):
                ag(d, k, e, 0).start()
        for e in range(4):
            pf(k, e, 0).start()

    def ag_step(k, t):
        for e in range(4):
            for d in range(2):
                if travels(d, e, t):
                    ag(d, k, e, t).wait_recv()
                    pf(k, e, t + 1 if d == 0 else 7 - t).start()
                    if travels(d, e, t + 1):
                        ag(d, k, e, t + 1).start()

    def ag_end(k):
        take(G.at[k, pl.ds(0, 8)], pf_r.at[k])

    def prep_a(part):
        def body(i, carry):
            rows = pl.ds(pl.multiple_of(i * 64, 64), 64)
            top, low = split(-A32[rows, :])
            Ah[rows, :] = top
            Al[rows, :] = low
            return carry

        lax.fori_loop(4 * part, 4 * part + 4, body, 0)

    def prep_c():
        def body(i, carry):
            for m in range(3):
                top, low = split(jnp.transpose(C32[m, :, lanes(i, 128)]))
                rows = pl.ds(pl.multiple_of(i * 128, 128), 128)
                Ch[m, rows, :] = top
                Cl[m, rows, :] = low
            return carry

        lax.fori_loop(0, 4, body, 0)

    def triple(left, top, low, dims=NN):
        n = left.shape[0]
        a, b = split(left)
        wide = dot(jnp.concatenate([a, b], 0), top, dims)
        return wide[0:n] + wide[n:] + dot(a, low, dims)

    def prep_d():
        own = pl.ds(pl.multiple_of(c * 32, 32), 32)
        c0p, c1p, c2p = (Ch[m, own, :].astype(F32) + Cl[m, own, :].astype(F32) for m in range(3))
        d0, d1, d2 = D32[0, own, :], D32[1, own, :], D32[2, own, :]
        u02p = triple(c2p, Ch[0], Cl[0]) - c1p
        t0 = jnp.concatenate([d0, triple(jnp.concatenate([-c0p, u02p], 0), *split(D32[0]))], 0)
        t1 = triple(-c2p, *split(D32[1]))
        zero = jnp.zeros_like(d0)
        v1 = jnp.concatenate([zero, d1, t1], 0) - triple(t0, Ch[0], Cl[0], NT)
        v2 = jnp.concatenate([zero, zero, d2], 0) - triple(t0, Ch[1], Cl[1], NT) - triple(v1, Ch[2], Cl[2], NT)
        VD[0] = d0
        VD[1] = v1[0:32]
        VD[2] = v2[0:32]
        VD[3] = v1[32:64]
        VD[4] = v2[32:64]
        VD[5] = v2[64:96]

    def comp_r(k, l, lo, hi):
        m = k + l - 1

        def body(j, carry):
            here = lanes(j, 256)
            value = jnp.zeros((512, 256), F32) if l == 0 else RM[k - 1, :, here]
            for h in range(2):
                deep = pl.ds(256 * h, 256)
                top, low = HS[l, h, pl.ds(0, 256), here], HS[l, h, pl.ds(256, 256), here]
                left = Ch[m, :, deep]
                value = value + (dot(left, top) + dot(Cl[m, :, deep], top) + dot(left, low))
            RM[k - 1, :, here] = value
            return carry

        lax.fori_loop(lo, hi, body, 0)

    def comp_h(k):
        def body(j, carry):
            here = lanes(j, 256)
            first = flags[k, r * 8 + 2 * j].astype(F32)
            second = flags[k, r * 8 + 2 * j + 1].astype(F32)
            mask = jnp.where(lax.broadcasted_iota(jnp.int32, (1, 256), 1) < 128, first, second)
            value = G[k, :, :, here].reshape(512, 256) * mask
            if k > 0:
                value = value - RM[k - 1, :, here]
            top, low = split(value)
            for h in range(2):
                HS[k, h, pl.ds(0, 256), here] = top[256 * h : 256 * h + 256]
                HS[k, h, pl.ds(256, 256), here] = low[256 * h : 256 * h + 256]
            return carry

        lax.fori_loop(0, 4, body, 0)

    def product(k, half, j):
        here = lanes(j, 256)
        wide = dot(HS[k, half], Ah[:, here])
        value = wide[0:256] + wide[256:512] + dot(HS[k, half, pl.ds(0, 256), :], Al[:, here])
        value = value.reshape(8, 4, 8, 256)
        if half == 1:
            PYY[k, j] = value
        else:
            for i in range(4):
                PXX[k, i, :, :, here] = value[:, i]

    def comp_all(k, lo, hi):
        def body(j, carry):
            product(k, 0, j)
            product(k, 1, j)
            return carry

        lax.fori_loop(lo, hi, body, 0)

    def comp_p(k, half, lo, hi):
        def body(j, carry):
            product(k, half, j)
            return carry

        lax.fori_loop(lo, hi, body, 0)

    class Ring:
        def __init__(self, k, phase, own, relay, final, me, device, out):
            self.own, self.relay, self.final, self.me, self.out = own, relay, final, me, out
            right, left = device((me + 1) % 4), device((me + 3) % 4)
            self.next, self.prev, self.far = (me + 1) % 4, (me + 3) % 4, (me + 2) % 4
            lower, upper = pl.ds(0, 4), pl.ds(4, 4)
            self.done = rs_r.at[k, phase, 2]
            sem = lambda i: (sent.at[2], rs_r.at[k, phase, i])
            self.relay_r = remote(own(self.far, 0), relay.at[0], *sem(0), right)
            self.relay_l = remote(own(self.far, 1), relay.at[1], *sem(1), left)
            self.raw_r = remote(own(self.next, 1), final.at[0, upper], *sem(2), right)
            self.raw_l = remote(own(self.prev, 0), final.at[1, lower], *sem(2), left)
            self.sum_r = remote(relay.at[0], final.at[0, lower], *sem(2), right)
            self.sum_l = remote(relay.at[1], final.at[1, upper], *sem(2), left)

        def start(self):
            self.relay_r.start()
            self.relay_l.start()

        def raw(self):
            self.raw_r.start()
            self.raw_l.start()

        def mid(self):
            for side, copy, chunk, onward in (
                (0, self.relay_r, self.next, self.sum_r),
                (1, self.relay_l, self.prev, self.sum_l),
            ):
                copy.wait_recv()
                mine = self.own(chunk, side)

                def body(i, carry):
                    self.relay[side, i] = self.relay[side, i] + mine[i]
                    return carry

                lax.fori_loop(0, 4, body, 0)
                onward.start()

        def end(self):
            take(self.final, self.done)
            for side in range(2):
                mine = self.own(self.me, side)
                into = self.out(side)

                def body(i, carry):
                    into[i] = mine[i] + self.final[0, 4 * side + i] + self.final[1, 4 * side + i]
                    return carry

                lax.fori_loop(0, 4, body, 0)

    along_x = lambda t: {"prow": t * 4 + y}
    along_y = lambda t: {"prow": x * 4 + t}

    def rings(k):
        def parts(base, h):
            return pl.ds(base + 4 * h, 4)

        own_x1 = lambda t, h: PXX.at[k, t, parts(0, h)]
        own_y1 = lambda t, h: PYY.at[k, t, parts(0, h)]
        own_x2 = lambda t, h: PXX.at[k, x, parts(0, h), :, lanes(t, 256)]
        own_y2 = lambda t, h: PYY.at[k, y, parts(0, h), t]
        first = (
            Ring(k, 0, own_x1, RLX.at[k], FNX.at[k], x, along_x, lambda h: own_x1(x, h)),
            Ring(k, 1, own_y1, RLY.at[k], FNY.at[k], y, along_y, lambda h: own_y1(y, h)),
        )
        second = (
            Ring(k, 2, own_x2, RLX2.at[k], FNX2.at[k], y, along_y, lambda h: XS.at[parts(0, h), k]),
            Ring(k, 3, own_y2, RLY2.at[k], FNY2.at[k], x, along_x, lambda h: XS.at[parts(8, h), k]),
        )
        return first, second

    ring = [rings(k) for k in range(3)]

    def rs_start(k, phase, *which):
        for i in which or (0, 1):
            ring[k][phase][i].start()

    def rs_raw(k, phase, *which):
        for i in which or (0, 1):
            ring[k][phase][i].raw()

    def rs_mid(k, phase, *which):
        for i in which or (0, 1):
            ring[k][phase][i].mid()

    def rs_end(k, phase, *which):
        for i in which or (0, 1):
            ring[k][phase][i].end()

    plane = sorted(
        ((i, j) for i in range(4) for j in range(4) if i or j),
        key=lambda p: -(min(p[0], 4 - p[0]) + min(p[1], 4 - p[1])),
    )

    def begin(copy):
        for o in range(1, 16):
            copy(o).start()

    def partner(o):
        i, j = plane[o - 1]
        return (x + i) % 4, (y + j) % 4

    def za(k):
        def copy(o):
            to = (c + 8 + (o // 2) * (2 * (o % 2) - 1)) % 16
            return remote(XS.at[to, k], ZB.at[c, k], sent.at[3], za_r.at[k], {"pcol": to})

        return copy

    def xa(k):
        def copy(o):
            px, py = partner(o)
            to = px * 4 + py
            return remote(
                ZB.at[to, k], XF.at[k, x, :, lanes(y, 256)], sent.at[4], xa_r.at[k], {"prow": to}
            )

        return copy

    def za_start(k):
        begin(za(k))
        ZB[c, k] = XS[c, k]

    def xa_start(k):
        take(ZB.at[pl.ds(0, 15), k], za_r.at[k])
        begin(xa(k))
        XF[k, x, :, lanes(y, 256)] = ZB[r, k]

    def xa_end(k):
        take(ZB.at[pl.ds(0, 15), k], xa_r.at[k])

    IN, RB, OU = (IN0, IN1, IN2), (RB0, RB1, RB2), (OU0, OU1, OU2)

    def inner(k):
        value = XF[k].reshape(32, 1024)
        xt_out[k] = value
        top, low = split(value)
        both = jnp.concatenate([top, low], 0)
        for m in range(k, 3):
            for h in range(2):
                wide = dot(both, HS[m, h, pl.ds(0, 256), :], NT)
                total = wide[0:32] + wide[32:64] + dot(top, HS[m, h, pl.ds(256, 256), :], NT)
                IN[k][:, :, pl.ds((m - k) * 512 + 256 * h, 256)] = total.reshape(4, 8, 256)

    def ra(k):
        w = 128 * (3 - k)

        def copy(o):
            px, py = partner(o)
            return remote(
                IN[k].at[px, :, lanes(py, w)], RB[k].at[o], sent.at[5], ra_r.at[k], {"prow": px * 4 + py}
            )

        return copy

    def ga(k):
        w = 128 * (3 - k)
        mine = OU[k].at[x, :, lanes(y, w)]

        def copy(o):
            px, py = partner(o)
            return remote(mine, mine, sent.at[6], ga_r.at[k], {"prow": px * 4 + py})

        return copy

    def ar_start(k):
        inner(k)
        begin(ra(k))

    def ar_mid(k):
        w = 128 * (3 - k)
        take(RB[k].at[pl.ds(1, 15)], ra_r.at[k])
        total = IN[k][x, :, lanes(y, w)]
        for o in range(1, 16):
            total = total + RB[k][o]
        OU[k][x, :, lanes(y, w)] = total
        begin(ga(k))

    def ar_end(k):
        take(RB[k].at[pl.ds(1, 15)], ga_r.at[k])
        places = (((yd_out, 0), (xc_out, 0), (xc_out, 1)), ((yd_out, 1), (xc_out, 2)), ((yd_out, 2),))[k]
        first = (0, 3, 5)[k]
        for i, (target, slot) in enumerate(places):
            got = OU[k][:, :, pl.ds(i * 512, 512)].reshape(32, 512)
            target[slot] = VD[first + i] - got

    load_pan.wait()
    ag_start(0)
    load_a.start()
    load_c.start()
    load_d.start()
    load_f.start()
    ag_step(0, 0)
    load_a.wait()
    prep_a(0)
    prep_a(1)
    prep_a(2)
    prep_a(3)
    load_c.wait()
    prep_c()
    ag_step(0, 1)
    ag_start(1)
    load_d.wait()
    load_f.wait()
    prep_d()
    ag_step(0, 2)
    ag_step(1, 0)
    ag_step(0, 3)

    @pl.when(core == 1)
    def _():
        ag_step(1, 1)

    ag_start(2)
    ag_end(0)
    comp_h(0)
    comp_all(0, 0, 2)

    @pl.when(core == 0)
    def _():
        ag_step(1, 1)

    ag_step(2, 0)
    comp_all(0, 2, 4)
    rs_start(0, 0)
    ag_step(1, 2)
    comp_r(1, 0, 0, 2)
    rs_raw(0, 0)
    comp_r(1, 0, 2, 4)
    ag_step(2, 1)
    comp_r(2, 0, 0, 2)
    ag_step(1, 3)

    @pl.when(core == 1)
    def _():
        comp_r(2, 0, 2, 4)

    ag_end(1)
    comp_h(1)
    comp_all(1, 0, 2)
    rs_mid(0, 0)
    ag_step(2, 2)
    comp_all(1, 2, 4)
    rs_start(1, 0)

    @pl.when(core == 0)
    def _():
        comp_r(2, 0, 2, 4)

    rs_raw(1, 0)
    comp_r(2, 1, 0, 4)
    ag_step(2, 3)
    rs_end(0, 0)
    rs_start(0, 1)
    rs_raw(0, 1)
    ag_end(2)
    comp_h(2)
    comp_p(2, 0, 0, 2)
    rs_mid(1, 0)
    comp_p(2, 0, 2, 4)
    rs_start(2, 0, 0)
    comp_p(2, 1, 0, 2)
    rs_raw(2, 0, 0)
    comp_p(2, 1, 2, 4)
    rs_start(2, 0, 1)
    rs_raw(2, 0, 1)
    rs_mid(0, 1)
    rs_end(1, 0)
    rs_start(1, 1)
    rs_raw(1, 1)
    rs_mid(2, 0)
    rs_mid(1, 1)
    rs_end(2, 0, 0)
    rs_start(2, 1, 0)
    rs_raw(2, 1, 0)
    rs_end(2, 0, 1)
    rs_start(2, 1, 1)
    rs_raw(2, 1, 1)
    rs_end(0, 1)
    za_start(0)
    rs_end(1, 1)
    za_start(1)
    rs_mid(2, 1)
    rs_end(2, 1)
    za_start(2)
    xa_start(0)
    xa_start(1)
    xa_start(2)
    xa_end(0)
    ar_start(0)
    xa_end(1)
    ar_start(1)
    xa_end(2)
    ar_start(2)
    ar_mid(0)
    ar_mid(1)
    ar_mid(2)
    ar_end(0)
    ar_end(1)
    ar_end(2)

    for i, ref in enumerate((
        G.at[:, pl.ds(0, 7)], G.at[:, pl.ds(0, 8)], G.at[:, pl.ds(0, 15)],
        ZB.at[pl.ds(0, 15)], ZB.at[pl.ds(0, 15)], ZB.at[pl.ds(0, 15)], ZB.at[pl.ds(0, 15)],
    )):
        take(ref, sent.at[i])


def finish(xt, xc, yd, xt_out, xc_out, yd_out, a, b, c, inward, outward):
    trips = []
    for i, (source, held, target) in enumerate(((xt, a, xt_out), (xc, b, xc_out), (yd, c, yd_out))):
        arrive = pltpu.make_async_copy(source, held, inward.at[i])
        arrive.start()
        trips.append((arrive, pltpu.make_async_copy(held, target, outward.at[i])))
    for arrive, leave in trips:
        arrive.wait()
        leave.start()
    for arrive, leave in trips:
        leave.wait()


def scratch():
    v = pltpu.VMEM
    sem = pltpu.SemaphoreType.DMA
    return [
        v((3, 16, 32, 1024), F32), v((3, 2, 512, 1024), BF16), pltpu.SMEM((3, 128), jnp.int32),
        v((1024, 1024), F32), v((1024, 1024), BF16), v((1024, 1024), BF16),
        v((3, 512, 512), F32), v((3, 512, 512), F32), v((3, 512, 512), BF16), v((3, 512, 512), BF16),
        v((2, 512, 1024), F32),
        v((3, 4, 8, 8, 1024), F32), v((3, 4, 8, 4, 8, 256), F32),
        v((3, 2, 4, 8, 1024), F32), v((3, 2, 8, 8, 1024), F32),
        v((3, 2, 4, 4, 8, 256), F32), v((3, 2, 8, 4, 8, 256), F32),
        v((3, 2, 4, 8, 256), F32), v((3, 2, 8, 8, 256), F32),
        v((3, 2, 4, 8, 256), F32), v((3, 2, 8, 8, 256), F32),
        v((16, 3, 8, 256), F32), v((16, 3, 8, 256), F32), v((3, 4, 8, 1024), F32),
        v((4, 8, 1536), F32), v((4, 8, 1024), F32), v((4, 8, 512), F32),
        v((16, 8, 384), F32), v((16, 8, 256), F32), v((16, 8, 128), F32),
        v((4, 8, 1536), F32), v((4, 8, 1024), F32), v((4, 8, 512), F32),
        v((6, 32, 512), F32),
        sem((5,)), sem((2, 3, 4, 4)), sem((3,)), sem((3, 4, 3)),
        sem((3,)), sem((3,)), sem((3,)), sem((3,)), sem((7,)),
    ]


def shards(ainv, panels, pattern, coupling, dinv):
    any_space = pl.BlockSpec(memory_space=pl.ANY)
    vmem = pl.BlockSpec(memory_space=pltpu.VMEM)
    shapes = ((3, 32, 1024), (3, 32, 512), (3, 32, 512))
    results = tuple(jax.ShapeDtypeStruct(shape, F32) for shape in shapes)
    held = pl.pallas_call(
        kernel,
        out_shape=results,
        in_specs=[any_space] * 5,
        out_specs=(vmem, vmem, vmem),
        scratch_shapes=scratch(),
        compiler_params=pltpu.CompilerParams(
            collective_id=0, has_side_effects=True, vmem_limit_bytes=64 * 1024 * 1024 - 65536
        ),
    )(jnp.swapaxes(panels, 1, 2), pattern, coupling, dinv, ainv)
    xt, xc, yd = pl.pallas_call(
        finish,
        out_shape=results,
        in_specs=[any_space] * 3,
        out_specs=(any_space,) * 3,
        scratch_shapes=[pltpu.VMEM(shape, F32) for shape in shapes] + [pltpu.SemaphoreType.DMA((3,))] * 2,
    )(*held)
    return jnp.swapaxes(xt, 1, 2), xc, yd


def solution(mesh):
    placed = (P("prow", "pcol"), P(None, "prow", "pcol"), P(), P(), P())
    return jax.shard_map(
        shards,
        mesh=mesh,
        in_specs=placed,
        out_specs=(P(None, "prow", "pcol"), P(None, "pcol", None), P(None, "pcol", None)),
        check_vma=False,
    )
```

```python
import jax
import jax.numpy as jnp
from jax import lax
from jax.experimental import pallas as pl
from jax.experimental.pallas import tpu as pltpu
from jax.sharding import PartitionSpec as P

NB = 128
F32 = jnp.float32
BF16 = jnp.bfloat16
MESH = pl.DeviceIdType.MESH

NN = (((1,), (0,)), ((), ()))
NT = (((1,), (1,)), ((), ()))


def split(value):
    top = value.astype(BF16)
    return top, (value - top.astype(F32)).astype(BF16)


def dot(left, right, dims=NN):
    return lax.dot_general(left, right, dims, preferred_element_type=F32)


def lanes(index, size):
    return pl.ds(pl.multiple_of(index * size, 128), size)


def kernel(
    pan, pat, coup, dinv, ainv, xt_out, xc_out, yd_out,
    G, HS, flags, A32, Ah, Al, C32, D32, Ch, Cl, RM, PXX, PYY,
    RLX, FNX, RLY, FNY, RLX2, FNX2, RLY2, FNY2, FD,
    XS, ZB, XF, IN0, IN1, IN2, RB0, RB1, RB2, OU0, OU1, OU2, VD,
    load_sem, ag_r, pf_r, rs_r, za_r, xa_r, ra_r, ga_r, sent,
):
    r = lax.axis_index("prow")
    c = lax.axis_index("pcol")
    x, y = r // 4, r % 4
    z, core = c // 2, c % 2

    load_pan = pltpu.make_async_copy(pan, G.at[:, c], load_sem.at[0])
    load_a = pltpu.make_async_copy(ainv, A32, load_sem.at[1])
    load_c = pltpu.make_async_copy(coup, C32, load_sem.at[2])
    load_d = pltpu.make_async_copy(dinv, D32, load_sem.at[3])
    load_f = pltpu.make_async_copy(pat, flags, load_sem.at[4])
    load_pan.start()

    barrier = pltpu.get_barrier_semaphore()

    for near in (2 * ((z + 1) % 8) + core, 2 * ((z + 7) % 8) + core, 2 * z + 1 - core):
        pl.semaphore_signal(barrier, inc=1, device_id={"pcol": near}, device_id_type=MESH)
    for near in (x * 4 + (y + 1) % 4, x * 4 + (y + 3) % 4, (x + 1) % 4 * 4 + y, (x + 3) % 4 * 4 + y):
        pl.semaphore_signal(barrier, inc=1, device_id={"prow": near}, device_id_type=MESH)
    pl.semaphore_wait(barrier, 7)

    def remote(src, dst, send, recv, device):
        return pltpu.make_async_remote_copy(
            src_ref=src, dst_ref=dst, send_sem=send, recv_sem=recv, device_id=device, device_id_type=MESH
        )

    def take(ref, semaphore):
        pltpu.make_async_copy(ref, ref, semaphore).wait()

    def ag(d, k, e, t):
        chip = (z + 8 - t) % 8 if d == 0 else (z + t) % 8
        near = (z + 1) % 8 if d == 0 else (z + 7) % 8
        part = G.at[k, 2 * chip + core, pl.ds(8 * e, 8)]
        return remote(part, part, sent.at[0], ag_r.at[d, k, e, t], {"pcol": 2 * near + core})

    def pf(k, e, q):
        part = G.at[k, 2 * ((z + 8 - q) % 8) + core, pl.ds(8 * e, 8)]
        return remote(part, part, sent.at[1], pf_r.at[k], {"pcol": 2 * z + 1 - core})

    def travels(d, e, t):
        return t < 3 or (t == 3 and d == e // 2)

    def ag_start(k):
        for e in range(4):
            for d in range(2):
                ag(d, k, e, 0).start()
        for e in range(4):
            pf(k, e, 0).start()

    def ag_step(k, t):
        for e in range(4):
            for d in range(2):
                if travels(d, e, t):
                    ag(d, k, e, t).wait_recv()
                    pf(k, e, t + 1 if d == 0 else 7 - t).start()
                    if travels(d, e, t + 1):
                        ag(d, k, e, t + 1).start()

    def ag_end(k):
        take(G.at[k, pl.ds(0, 8)], pf_r.at[k])

    def prep_a(part):
        def body(i, carry):
            rows = pl.ds(pl.multiple_of(i * 64, 64), 64)
            top, low = split(-A32[rows, :])
            Ah[rows, :] = top
            Al[rows, :] = low
            return carry

        lax.fori_loop(4 * part, 4 * part + 4, body, 0)

    def prep_c():
        def body(i, carry):
            for m in range(3):
                top, low = split(jnp.transpose(C32[m, :, lanes(i, 128)]))
                rows = pl.ds(pl.multiple_of(i * 128, 128), 128)
                Ch[m, rows, :] = top
                Cl[m, rows, :] = low
            return carry

        lax.fori_loop(0, 4, body, 0)

    def triple(left, top, low, dims=NN):
        n = left.shape[0]
        a, b = split(left)
        wide = dot(jnp.concatenate([a, b], 0), top, dims)
        return wide[0:n] + wide[n:] + dot(a, low, dims)

    def prep_d():
        own = pl.ds(pl.multiple_of(c * 32, 32), 32)
        c0p, c1p, c2p = (Ch[m, own, :].astype(F32) + Cl[m, own, :].astype(F32) for m in range(3))
        d0, d1, d2 = D32[0, own, :], D32[1, own, :], D32[2, own, :]
        u02p = triple(c2p, Ch[0], Cl[0]) - c1p
        t0 = jnp.concatenate([d0, triple(jnp.concatenate([-c0p, u02p], 0), *split(D32[0]))], 0)
        t1 = triple(-c2p, *split(D32[1]))
        zero = jnp.zeros_like(d0)
        v1 = jnp.concatenate([zero, d1, t1], 0) - triple(t0, Ch[0], Cl[0], NT)
        v2 = jnp.concatenate([zero, zero, d2], 0) - triple(t0, Ch[1], Cl[1], NT) - triple(v1, Ch[2], Cl[2], NT)
        VD[0] = d0
        VD[1] = v1[0:32]
        VD[2] = v2[0:32]
        VD[3] = v1[32:64]
        VD[4] = v2[32:64]
        VD[5] = v2[64:96]

    def comp_r(k, l, lo, hi):
        m = k + l - 1

        def body(j, carry):
            here = lanes(j, 256)
            value = jnp.zeros((512, 256), F32) if l == 0 else RM[k - 1, :, here]
            for h in range(2):
                deep = pl.ds(256 * h, 256)
                top, low = HS[l, h, pl.ds(0, 256), here], HS[l, h, pl.ds(256, 256), here]
                left = Ch[m, :, deep]
                value = value + (dot(left, top) + dot(Cl[m, :, deep], top) + dot(left, low))
            RM[k - 1, :, here] = value
            return carry

        lax.fori_loop(lo, hi, body, 0)

    def comp_h(k):
        def body(j, carry):
            here = lanes(j, 256)
            first = flags[k, r * 8 + 2 * j].astype(F32)
            second = flags[k, r * 8 + 2 * j + 1].astype(F32)
            mask = jnp.where(lax.broadcasted_iota(jnp.int32, (1, 256), 1) < 128, first, second)
            value = G[k, :, :, here].reshape(512, 256) * mask
            if k > 0:
                value = value - RM[k - 1, :, here]
            top, low = split(value)
            for h in range(2):
                HS[k, h, pl.ds(0, 256), here] = top[256 * h : 256 * h + 256]
                HS[k, h, pl.ds(256, 256), here] = low[256 * h : 256 * h + 256]
            return carry

        lax.fori_loop(0, 4, body, 0)

    def product(k, half, j):
        here = lanes(j, 256)
        wide = dot(HS[k, half], Ah[:, here])
        value = wide[0:256] + wide[256:512] + dot(HS[k, half, pl.ds(0, 256), :], Al[:, here])
        value = value.reshape(8, 4, 8, 256)
        if half == 1:
            PYY[k, j] = value
        else:
            for i in range(4):
                PXX[k, i, :, :, here] = value[:, i]

    def comp_all(k, lo, hi):
        def body(j, carry):
            product(k, 0, j)
            product(k, 1, j)
            return carry

        lax.fori_loop(lo, hi, body, 0)

    def comp_p(k, half, lo, hi):
        def body(j, carry):
            product(k, half, j)
            return carry

        lax.fori_loop(lo, hi, body, 0)

    class Ring:
        def __init__(self, k, phase, own, relay, final, me, device, out):
            self.own, self.relay, self.final, self.me, self.out = own, relay, final, me, out
            right, left = device((me + 1) % 4), device((me + 3) % 4)
            self.next, self.prev, self.far = (me + 1) % 4, (me + 3) % 4, (me + 2) % 4
            lower, upper = pl.ds(0, 4), pl.ds(4, 4)
            self.done = rs_r.at[k, phase, 2]
            sem = lambda i: (sent.at[2], rs_r.at[k, phase, i])
            self.relay_r = remote(own(self.far, 0), relay.at[0], *sem(0), right)
            self.relay_l = remote(own(self.far, 1), relay.at[1], *sem(1), left)
            self.raw_r = remote(own(self.next, 1), final.at[0, upper], *sem(2), right)
            self.raw_l = remote(own(self.prev, 0), final.at[1, lower], *sem(2), left)
            self.sum_r = remote(relay.at[0], final.at[0, lower], *sem(2), right)
            self.sum_l = remote(relay.at[1], final.at[1, upper], *sem(2), left)

        def start(self):
            self.relay_r.start()
            self.relay_l.start()

        def raw(self):
            self.raw_r.start()
            self.raw_l.start()

        def mid(self):
            for side, copy, chunk, onward in (
                (0, self.relay_r, self.next, self.sum_r),
                (1, self.relay_l, self.prev, self.sum_l),
            ):
                copy.wait_recv()
                mine = self.own(chunk, side)

                def body(i, carry):
                    self.relay[side, i] = self.relay[side, i] + mine[i]
                    return carry

                lax.fori_loop(0, 4, body, 0)
                onward.start()

        def end(self):
            take(self.final, self.done)
            for side in range(2):
                mine = self.own(self.me, side)
                into = self.out(side)

                def body(i, carry):
                    into[i] = mine[i] + self.final[0, 4 * side + i] + self.final[1, 4 * side + i]
                    return carry

                lax.fori_loop(0, 4, body, 0)

    class Direct:
        def __init__(self, k, phase, own, held, me, device, out):
            self.own, self.held, self.me, self.out, self.done = own, held, me, out, rs_r.at[k, phase, 2]
            self.copies = []
            for i, step in enumerate((2, 1, 3)):
                to = (me + step) % 4
                self.copies.append(remote(own(to, None), held.at[i], sent.at[2], self.done, device(to)))

        def start(self):
            for copy in self.copies:
                copy.start()

        def end(self):
            take(self.held, self.done)
            mine, into = self.own(self.me, None), self.out(None)

            def body(i, carry):
                into[i] = mine[i] + self.held[0, i] + self.held[1, i] + self.held[2, i]
                return carry

            lax.fori_loop(0, 8, body, 0)

    along_x = lambda t: {"prow": t * 4 + y}
    along_y = lambda t: {"prow": x * 4 + t}

    def rings(k):
        def parts(base, h):
            return pl.ds(base, 8) if h is None else pl.ds(base + 4 * h, 4)

        own_x1 = lambda t, h: PXX.at[k, t, parts(0, h)]
        own_y1 = lambda t, h: PYY.at[k, t, parts(0, h)]
        own_x2 = lambda t, h: PXX.at[k, x, parts(0, h), :, lanes(t, 256)]
        own_y2 = lambda t, h: PYY.at[k, y, parts(0, h), t]
        first = (
            Ring(k, 0, own_x1, RLX.at[k], FNX.at[k], x, along_x, lambda h: own_x1(x, h)),
            Ring(k, 1, own_y1, RLY.at[k], FNY.at[k], y, along_y, lambda h: own_y1(y, h)),
        )
        second = (
            Ring(k, 2, own_x2, RLX2.at[k], FNX2.at[k], y, along_y, lambda h: XS.at[parts(0, h), k]),
            Ring(k, 3, own_y2, RLY2.at[k], FNY2.at[k], x, along_x, lambda h: XS.at[parts(8, h), k]),
        )
        if k == 2:
            second = (
                Direct(k, 2, own_x2, FD.at[0], y, along_y, lambda h: XS.at[parts(0, h), k]),
                Direct(k, 3, own_y2, FD.at[1], x, along_x, lambda h: XS.at[parts(8, h), k]),
            )
        return first, second

    ring = [rings(k) for k in range(3)]

    def rs_start(k, phase, *which):
        for i in which or (0, 1):
            ring[k][phase][i].start()

    def rs_raw(k, phase, *which):
        for i in which or (0, 1):
            ring[k][phase][i].raw()

    def rs_mid(k, phase, *which):
        for i in which or (0, 1):
            ring[k][phase][i].mid()

    def rs_end(k, phase, *which):
        for i in which or (0, 1):
            ring[k][phase][i].end()

    plane = sorted(
        ((i, j) for i in range(4) for j in range(4) if i or j),
        key=lambda p: -(min(p[0], 4 - p[0]) + min(p[1], 4 - p[1])),
    )

    def begin(copy):
        for o in range(1, 16):
            copy(o).start()

    def partner(o):
        i, j = plane[o - 1]
        return (x + i) % 4, (y + j) % 4

    def za(k):
        def copy(o):
            to = (c + 8 + (o // 2) * (2 * (o % 2) - 1)) % 16
            return remote(XS.at[to, k], ZB.at[c, k], sent.at[3], za_r.at[k], {"pcol": to})

        return copy

    def xa(k):
        def copy(o):
            px, py = partner(o)
            to = px * 4 + py
            return remote(
                ZB.at[to, k], XF.at[k, x, :, lanes(y, 256)], sent.at[4], xa_r.at[k], {"prow": to}
            )

        return copy

    def za_start(k):
        begin(za(k))
        ZB[c, k] = XS[c, k]

    def xa_start(k):
        take(ZB.at[pl.ds(0, 15), k], za_r.at[k])
        begin(xa(k))
        XF[k, x, :, lanes(y, 256)] = ZB[r, k]

    def xa_end(k):
        take(ZB.at[pl.ds(0, 15), k], xa_r.at[k])

    IN, RB, OU = (IN0, IN1, IN2), (RB0, RB1, RB2), (OU0, OU1, OU2)

    def inner(k):
        value = XF[k].reshape(32, 1024)
        xt_out[k] = value
        top, low = split(value)
        both = jnp.concatenate([top, low], 0)
        for m in range(k, 3):
            for h in range(2):
                wide = dot(both, HS[m, h, pl.ds(0, 256), :], NT)
                total = wide[0:32] + wide[32:64] + dot(top, HS[m, h, pl.ds(256, 256), :], NT)
                IN[k][:, :, pl.ds((m - k) * 512 + 256 * h, 256)] = total.reshape(4, 8, 256)

    def ra(k):
        w = 128 * (3 - k)

        def copy(o):
            px, py = partner(o)
            return remote(
                IN[k].at[px, :, lanes(py, w)], RB[k].at[o], sent.at[5], ra_r.at[k], {"prow": px * 4 + py}
            )

        return copy

    def ga(k):
        w = 128 * (3 - k)
        mine = OU[k].at[x, :, lanes(y, w)]

        def copy(o):
            px, py = partner(o)
            return remote(mine, mine, sent.at[6], ga_r.at[k], {"prow": px * 4 + py})

        return copy

    def ar_start(k):
        inner(k)
        begin(ra(k))

    def ar_mid(k):
        w = 128 * (3 - k)
        take(RB[k].at[pl.ds(1, 15)], ra_r.at[k])
        total = IN[k][x, :, lanes(y, w)]
        for o in range(1, 16):
            total = total + RB[k][o]
        OU[k][x, :, lanes(y, w)] = total
        begin(ga(k))

    def ar_end(k):
        take(RB[k].at[pl.ds(1, 15)], ga_r.at[k])
        places = (((yd_out, 0), (xc_out, 0), (xc_out, 1)), ((yd_out, 1), (xc_out, 2)), ((yd_out, 2),))[k]
        first = (0, 3, 5)[k]
        for i, (target, slot) in enumerate(places):
            got = OU[k][:, :, pl.ds(i * 512, 512)].reshape(32, 512)
            target[slot] = VD[first + i] - got

    load_pan.wait()
    ag_start(0)
    load_a.start()
    load_c.start()
    load_d.start()
    load_f.start()
    ag_step(0, 0)
    load_a.wait()
    prep_a(0)
    prep_a(1)
    prep_a(2)
    prep_a(3)
    load_c.wait()
    prep_c()
    ag_step(0, 1)
    ag_start(1)
    load_d.wait()
    load_f.wait()
    prep_d()
    ag_step(0, 2)
    ag_step(1, 0)
    ag_step(0, 3)

    @pl.when(core == 1)
    def _():
        ag_step(1, 1)

    ag_start(2)
    ag_end(0)
    comp_h(0)
    comp_all(0, 0, 2)

    @pl.when(core == 0)
    def _():
        ag_step(1, 1)

    ag_step(2, 0)
    comp_all(0, 2, 4)
    rs_start(0, 0)
    ag_step(1, 2)
    comp_r(1, 0, 0, 2)
    rs_raw(0, 0)
    comp_r(1, 0, 2, 4)
    ag_step(2, 1)
    comp_r(2, 0, 0, 2)
    ag_step(1, 3)

    @pl.when(core == 1)
    def _():
        comp_r(2, 0, 2, 4)

    ag_end(1)
    comp_h(1)
    comp_all(1, 0, 2)
    rs_mid(0, 0)
    ag_step(2, 2)
    comp_all(1, 2, 4)
    rs_start(1, 0)

    @pl.when(core == 0)
    def _():
        comp_r(2, 0, 2, 4)

    rs_raw(1, 0)
    comp_r(2, 1, 0, 4)
    ag_step(2, 3)
    rs_end(0, 0)
    rs_start(0, 1)
    rs_raw(0, 1)
    ag_end(2)
    comp_h(2)
    comp_p(2, 0, 0, 2)
    rs_mid(1, 0)
    comp_p(2, 0, 2, 4)
    rs_start(2, 0, 0)
    comp_p(2, 1, 0, 2)
    rs_raw(2, 0, 0)
    comp_p(2, 1, 2, 4)
    rs_start(2, 0, 1)
    rs_raw(2, 0, 1)
    rs_mid(0, 1)
    rs_end(1, 0)
    rs_start(1, 1)
    rs_raw(1, 1)
    rs_mid(2, 0)
    rs_mid(1, 1)
    rs_end(0, 1)
    za_start(0)
    rs_end(2, 0, 0)
    rs_start(2, 1, 0)
    rs_end(2, 0, 1)
    rs_start(2, 1, 1)
    rs_end(1, 1)
    za_start(1)
    rs_end(2, 1)
    za_start(2)
    xa_start(0)
    xa_start(1)
    xa_start(2)
    xa_end(0)
    ar_start(0)
    xa_end(1)
    ar_start(1)
    xa_end(2)
    ar_start(2)
    ar_mid(0)
    ar_mid(1)
    ar_mid(2)
    ar_end(0)
    ar_end(1)
    ar_end(2)

    for i, ref in enumerate((
        G.at[:, pl.ds(0, 7)], G.at[:, pl.ds(0, 8)], G.at[:, pl.ds(0, 15)],
        ZB.at[pl.ds(0, 15)], ZB.at[pl.ds(0, 15)], ZB.at[pl.ds(0, 15)], ZB.at[pl.ds(0, 15)],
    )):
        take(ref, sent.at[i])


def finish(xt, xc, yd, xt_out, xc_out, yd_out, a, b, c, inward, outward):
    trips = []
    for i, (source, held, target) in enumerate(((xt, a, xt_out), (xc, b, xc_out), (yd, c, yd_out))):
        arrive = pltpu.make_async_copy(source, held, inward.at[i])
        arrive.start()
        trips.append((arrive, pltpu.make_async_copy(held, target, outward.at[i])))
    for arrive, leave in trips:
        arrive.wait()
        leave.start()
    for arrive, leave in trips:
        leave.wait()


def scratch():
    v = pltpu.VMEM
    sem = pltpu.SemaphoreType.DMA
    return [
        v((3, 16, 32, 1024), F32), v((3, 2, 512, 1024), BF16), pltpu.SMEM((3, 128), jnp.int32),
        v((1024, 1024), F32), v((1024, 1024), BF16), v((1024, 1024), BF16),
        v((3, 512, 512), F32), v((3, 512, 512), F32), v((3, 512, 512), BF16), v((3, 512, 512), BF16),
        v((2, 512, 1024), F32),
        v((3, 4, 8, 8, 1024), F32), v((3, 4, 8, 4, 8, 256), F32),
        v((3, 2, 4, 8, 1024), F32), v((3, 2, 8, 8, 1024), F32),
        v((3, 2, 4, 4, 8, 256), F32), v((3, 2, 8, 4, 8, 256), F32),
        v((3, 2, 4, 8, 256), F32), v((3, 2, 8, 8, 256), F32),
        v((3, 2, 4, 8, 256), F32), v((3, 2, 8, 8, 256), F32),
        v((2, 3, 8, 8, 256), F32),
        v((16, 3, 8, 256), F32), v((16, 3, 8, 256), F32), v((3, 4, 8, 1024), F32),
        v((4, 8, 1536), F32), v((4, 8, 1024), F32), v((4, 8, 512), F32),
        v((16, 8, 384), F32), v((16, 8, 256), F32), v((16, 8, 128), F32),
        v((4, 8, 1536), F32), v((4, 8, 1024), F32), v((4, 8, 512), F32),
        v((6, 32, 512), F32),
        sem((5,)), sem((2, 3, 4, 4)), sem((3,)), sem((3, 4, 3)),
        sem((3,)), sem((3,)), sem((3,)), sem((3,)), sem((7,)),
    ]


def shards(ainv, panels, pattern, coupling, dinv):
    any_space = pl.BlockSpec(memory_space=pl.ANY)
    vmem = pl.BlockSpec(memory_space=pltpu.VMEM)
    shapes = ((3, 32, 1024), (3, 32, 512), (3, 32, 512))
    results = tuple(jax.ShapeDtypeStruct(shape, F32) for shape in shapes)
    held = pl.pallas_call(
        kernel,
        out_shape=results,
        in_specs=[any_space] * 5,
        out_specs=(vmem, vmem, vmem),
        scratch_shapes=scratch(),
        compiler_params=pltpu.CompilerParams(
            collective_id=0, has_side_effects=True, vmem_limit_bytes=64 * 1024 * 1024 - 65536
        ),
    )(jnp.swapaxes(panels, 1, 2), pattern, coupling, dinv, ainv)
    xt, xc, yd = pl.pallas_call(
        finish,
        out_shape=results,
        in_specs=[any_space] * 3,
        out_specs=(any_space,) * 3,
        scratch_shapes=[pltpu.VMEM(shape, F32) for shape in shapes] + [pltpu.SemaphoreType.DMA((3,))] * 2,
    )(*held)
    return jnp.swapaxes(xt, 1, 2), xc, yd


def solution(mesh):
    placed = (P("prow", "pcol"), P(None, "prow", "pcol"), P(), P(), P())
    return jax.shard_map(
        shards,
        mesh=mesh,
        in_specs=placed,
        out_specs=(P(None, "prow", "pcol"), P(None, "pcol", None), P(None, "pcol", None)),
        check_vma=False,
    )
```
